256 devices in a mesh: ctx: 32 (over z, x), tp: 8 (over y, core).
Axes of the slice: x: 4, y: 4, z: 8, core: 2. Of those that a mesh axis runs over, the one named last changes fastest.
Arguments:
- tokens: bfloat16 [8192, 2048], P(('ctx', 'tp')), may hold values from -6 to 6
- w_query_key: bfloat16 [2, 2048, 2048], P(None, None, 'tp'), may hold values from -0.125 to 0.125
- w_value: bfloat16 [2048, 4096], P(None, 'tp'), may hold values from -0.125 to 0.125
- w_gate_out: bfloat16 [2048, 4096], P(None, 'tp'), may hold values from -0.125 to 0.125
- conv_query_key: float32 [2, 4, 2048], P(None, None, 'tp'), may hold values from -3 to 3
- conv_value: float32 [4, 4096], P(None, 'tp'), may hold values from -3 to 3
- log_decay: float32 [32, 8192], P('tp', 'ctx'), as said below
- beta: float32 [32, 8192], P('tp', 'ctx'), as said below
- seg_start: int32 [8192], P('ctx'), may hold values from 0 to 8191, as said below
- norm_gain: float32 [128], replicated, may hold values from 0.1 to 1.9
- w_output: bfloat16 [4096, 2048], P('tp'), may hold values from -0.09375 to 0.09375
Outputs:
- mixed: bfloat16 [8192, 2048], P(('ctx', 'tp'))
The draws below stay inside these ranges and needn't reach their ends.
Inputs may be any that keep to these rules, and one draw needn't show every extreme that they name: seg_start never falls along the tokens, seg_start[t] <= t, and seg_start[t] == t exactly at the first token of each rollout; two to five rollouts, the last token opening one of its own. log_decay <= 0. 0 < beta < 1.
All inputs are finite; a program needn't handle non-finite values.
Results may differ from the reference program's by a relative error of at most 0.014.
Values may be sent and summed in bfloat16 or wider, within the bound.
No kernel may reach another device: no remote copies, remote signals or barrier semaphores. Data moves between devices by JAX's collectives and lax.ppermute only.
A program may use at most 64 MiB of HBM per device.

```python
import math
import jax
import jax.numpy as jnp
from jax import lax

D = 2048
HK = 16
DK = 128
VALUE_HEADS = 32
DV = 128
CONV = 4
STRETCH = 64
PACKED_TOKENS = 8192


def draw_log_decay(key, part):
    tier_key, variety_key, factor_key, locator_key, spike_run_key = jax.random.split(key, 5)
    slow_lo = math.log(0.1 / PACKED_TOKENS)
    slow_hi = math.log(1.0 / PACKED_TOKENS)
    slow = jnp.exp(jax.random.uniform(tier_key, (VALUE_HEADS, 1), jnp.float32, slow_lo, slow_hi))
    fast = jnp.exp(jax.random.uniform(variety_key, (VALUE_HEADS, 1), jnp.float32, math.log(1.0 / 50.0), math.log(1.0 / 20.0)))
    pick = jax.random.randint(jax.random.fold_in(variety_key, 7), (VALUE_HEADS, 1), 0, 2)
    tier_value = jnp.where(pick == 1, fast, slow)
    multiplier = jax.random.uniform(factor_key, (VALUE_HEADS, PACKED_TOKENS), jnp.float32, 0.5, 1.5)
    places = jax.random.randint(locator_key, (4,), 0, PACKED_TOKENS)
    matched_flag = jnp.any(jnp.arange(PACKED_TOKENS)[None, :] == places[:, None], axis=0)
    spike_run = jax.random.uniform(spike_run_key, (VALUE_HEADS, PACKED_TOKENS), jnp.float32, math.log(0.5), math.log(0.8))
    return (-tier_value * multiplier + jnp.where(matched_flag[None, :], spike_run, 0.0)).astype(jnp.float32)


def draw_beta(key, part):
    tier_key, factor_key = jax.random.split(key)
    tier_value = jnp.exp(jax.random.uniform(tier_key, (VALUE_HEADS, 1), jnp.float32, math.log(0.002), math.log(0.5)))
    multiplier = jax.random.uniform(factor_key, (VALUE_HEADS, PACKED_TOKENS), jnp.float32, 0.5, 1.5)
    return (tier_value * multiplier).astype(jnp.float32)


def draw_seg_start(key, part):
    random_cuts = jax.random.randint(key, (3,), 1, PACKED_TOKENS - 1)
    cuts = jnp.concatenate([random_cuts, jnp.full((1,), PACKED_TOKENS - 1, jnp.int32)]).astype(jnp.int32)
    position = jnp.arange(PACKED_TOKENS, dtype=jnp.int32)
    candidate = jnp.where(cuts[:, None] <= position[None, :], cuts[:, None], 0)
    return jnp.max(candidate, axis=0).astype(jnp.int32)


def block_levels(stream_key, dims, cuts, low, largest):
    loudness = 1.0
    for dim, parts in cuts:
        heights = jax.random.uniform(jax.random.fold_in(jax.random.fold_in(stream_key, 6), dim), (parts,), jnp.float32, low / len(cuts), largest / len(cuts))
        loudness = loudness * jnp.repeat(jnp.exp(heights), dims[dim] // parts).reshape((-1,) + (1,) * (len(dims) - 1 - dim))
    return loudness


def gaussian(rng, extent, deviation, limit, cuts=(), kind=jnp.bfloat16):
    loudness = block_levels(rng, extent, cuts, -0.22, 0.18) if cuts else 1.0
    values = jax.random.normal(rng, extent, jnp.float32) * deviation * loudness
    return jnp.minimum(jnp.maximum(values, -limit), limit).astype(kind)


def setup_inputs(seed: int = 0) -> dict:
    keys = jax.random.split(jax.random.key(seed), 12)
    return {
        "tokens": gaussian(keys[0], (PACKED_TOKENS, D), 1.0, 6.0, ((0, 256),)),
        "w_query_key": gaussian(keys[1], (2, D, HK * DK), D ** -0.5, 0.125, ((2, 8),)),
        "w_value": gaussian(keys[2], (D, VALUE_HEADS * DV), D ** -0.5, 0.125, ((1, 8),)),
        "w_gate_out": gaussian(keys[3], (D, VALUE_HEADS * DV), D ** -0.5, 0.125, ((1, 8),)),
        "conv_query_key": gaussian(keys[4], (2, CONV, HK * DK), 0.5, 3.0, ((2, 8),), jnp.float32),
        "conv_value": gaussian(keys[5], (CONV, VALUE_HEADS * DV), 0.5, 3.0, ((1, 8),), jnp.float32),
        "log_decay": draw_log_decay(jax.random.fold_in(keys[11], 71), 0),
        "beta": draw_beta(jax.random.fold_in(keys[11], 71), 0),
        "seg_start": draw_seg_start(jax.random.fold_in(keys[11], 71), 0),
        "norm_gain": jnp.clip(1.0 + 0.18 * jax.random.normal(keys[9], (DV,), jnp.float32), 0.1, 1.9),
        "w_output": gaussian(keys[10], (VALUE_HEADS * DV, D), (VALUE_HEADS * DV) ** -0.5, 0.09375, ((0, 8),)),
    }


highest = lax.Precision.HIGHEST

def stretch_parts(query, key, value, logd, betas, segs, first):
    size = segs.shape[0]
    gam = jnp.cumsum(logd, axis=-1)
    rows = jnp.arange(size)[:, None]
    cols = jnp.arange(size)[None, :]
    same = segs[:, None] == segs[None, :]
    within = jnp.logical_and(rows >= cols, same)
    strict = jnp.logical_and(rows > cols, same)
    gap = gam[:, :, None] - gam[:, None, :]
    decay = jnp.where(within, jnp.exp(jnp.where(within, gap, 0.0)), 0.0)
    lead = jnp.exp(gam) * (segs < first).astype(jnp.float32)
    keys_dot = jnp.einsum('hid,hjd->hij', key, key, precision=highest)
    lower_mat = jnp.eye(size, dtype=jnp.float32) + betas[:, :, None] * keys_dot * jnp.where(strict, decay, 0.0)
    w_one = lax.linalg.triangular_solve(lower_mat, betas[:, :, None] * value, left_side=True, lower=True, unit_diagonal=True)
    w_two = lax.linalg.triangular_solve(lower_mat, (betas * lead)[:, :, None] * key, left_side=True, lower=True, unit_diagonal=True)
    pmat = jnp.einsum('hid,hjd->hij', query, key, precision=highest) * decay
    local_out = jnp.einsum('hij,hjv->hiv', pmat, w_one, precision=highest)
    edge = lead[:, :, None] * query - jnp.einsum('hij,hjd->hid', pmat, w_two, precision=highest)
    tail = decay[:, -1, :]
    eye_key = jnp.eye(key.shape[-1], dtype=jnp.float32)
    mmat = lead[:, -1][:, None, None] * eye_key - jnp.einsum('hj,hjd,hje->hde', tail, w_two, key, precision=highest)
    bmat = jnp.einsum('hj,hjv,hjk->hvk', tail, w_one, key, precision=highest)
    return (local_out, edge, mmat, bmat)

def short_conv(pre, tail, weight, seg, position):
    extended = jnp.concatenate([tail, pre], axis=0).astype(jnp.float32)
    count = pre.shape[0]
    total = jnp.zeros((count, pre.shape[1]), jnp.float32)
    for j in range(CONV):
        reach = position - (CONV - 1) + j
        valid = (reach >= seg).astype(jnp.float32)[:, None]
        total = total + extended[j:j + count] * weight[j][None, :] * valid
    return jax.nn.silu(total)

def unit_norm(vecs):
    return vecs * lax.rsqrt(lax.optimization_barrier(jnp.sum(vecs * vecs, axis=-1, keepdims=True)) + 1e-06)

def reference(tokens, w_query_key, w_value, w_gate_out, conv_query_key, conv_value, log_decay, beta, seg_start, norm_gain, w_output):
    pre = jnp.concatenate([jnp.dot(tokens.astype(jnp.float32), w_query_key[0].astype(jnp.float32), preferred_element_type=jnp.float32), jnp.dot(tokens.astype(jnp.float32), w_query_key[1].astype(jnp.float32), preferred_element_type=jnp.float32), jnp.dot(tokens.astype(jnp.float32), w_value.astype(jnp.float32), preferred_element_type=jnp.float32)], axis=1).astype(jnp.bfloat16)
    gate_lin = jnp.dot(tokens.astype(jnp.float32), w_gate_out.astype(jnp.float32), preferred_element_type=jnp.float32)
    taps = jnp.concatenate([conv_query_key[0], conv_query_key[1], conv_value], axis=1)
    position = jnp.arange(PACKED_TOKENS, dtype=jnp.int32)
    empty_tail = jnp.zeros((CONV - 1, pre.shape[1]), jnp.bfloat16)
    act = short_conv(pre, empty_tail, taps, seg_start, position)
    width_qk = HK * DK
    query = unit_norm(act[:, :width_qk].reshape(PACKED_TOKENS, HK, DK)) * DK ** (-0.5)
    key = unit_norm(act[:, width_qk:2 * width_qk].reshape(PACKED_TOKENS, HK, DK))
    value = act[:, 2 * width_qk:].reshape(PACKED_TOKENS, VALUE_HEADS, DV)
    repeat = VALUE_HEADS // HK
    query = jnp.repeat(query, repeat, axis=1)
    key = jnp.repeat(key, repeat, axis=1)
    blocks = PACKED_TOKENS // STRETCH

    def arrange(field, depth):
        return field.reshape(blocks, STRETCH, VALUE_HEADS, depth).transpose(0, 2, 1, 3)
    logd = log_decay.reshape(VALUE_HEADS, blocks, STRETCH).transpose(1, 0, 2)
    betas = beta.reshape(VALUE_HEADS, blocks, STRETCH).transpose(1, 0, 2)
    segs = seg_start.reshape(blocks, STRETCH)
    firsts = (jnp.arange(blocks) * STRETCH).astype(jnp.int32)

    def advance(state, pieces):
        q_blk, k_blk, v_blk, l_blk, b_blk, s_blk, f_blk = pieces
        local_out, edge, mmat, bmat = stretch_parts(q_blk, k_blk, v_blk, l_blk, b_blk, s_blk, f_blk)
        result = local_out + jnp.einsum('hik,hvk->hiv', edge, state, precision=highest)
        state = jnp.einsum('hvk,hkl->hvl', state, mmat, precision=highest) + bmat
        return (state, result)
    start_state = jnp.zeros((VALUE_HEADS, DV, DK), jnp.float32)
    _, results = lax.scan(advance, start_state, (arrange(query, DK), arrange(key, DK), arrange(value, DV), logd, betas, segs, firsts))
    recur_out = results.transpose(0, 2, 1, 3).reshape(PACKED_TOKENS, VALUE_HEADS, DV)
    scale = lax.rsqrt(lax.optimization_barrier(jnp.mean(recur_out * recur_out, axis=-1, keepdims=True)) + 1e-06)
    normed = recur_out * scale * norm_gain * jax.nn.silu(gate_lin.reshape(PACKED_TOKENS, VALUE_HEADS, DV))
    normed = normed.reshape(PACKED_TOKENS, VALUE_HEADS * DV).astype(jnp.bfloat16)
    return jnp.dot(normed.astype(jnp.float32), w_output.astype(jnp.float32), preferred_element_type=jnp.float32).astype(jnp.bfloat16)
```

```python
import functools

import jax
import jax.numpy as jnp
from jax import lax
from jax.experimental import pallas as pl
from jax.experimental.pallas import tpu as pltpu
from jax.sharding import PartitionSpec as P


DK = 128
CONV = 4
T = 256
HALF = 128
PACK = 144
f32 = jnp.float32
bf16 = jnp.bfloat16
INTERPRET = False


def mm(a, b):
    return jnp.dot(a.astype(bf16), b.astype(bf16), preferred_element_type=f32)


def mm_exact(a, b):
    return jnp.dot(a, b, preferred_element_type=f32, precision=lax.Precision.HIGHEST)


def call(kernel, outs, scratch=(), smem=0, vmem=40, flops=0, name=None):
    def run(*args):
        in_specs = [
            pl.BlockSpec(memory_space=pltpu.SMEM if i < smem else pltpu.VMEM)
            for i in range(len(args))
        ]
        shapes = [jax.ShapeDtypeStruct(s, d) for s, d in outs]
        moved = sum(a.size * a.dtype.itemsize for a in args) + sum(
            s.size * s.dtype.itemsize for s in shapes
        )
        return pl.pallas_call(
            kernel,
            out_shape=shapes,
            in_specs=in_specs,
            out_specs=[pl.BlockSpec(memory_space=pltpu.VMEM)] * len(outs),
            scratch_shapes=list(scratch),
            compiler_params=pltpu.CompilerParams(vmem_limit_bytes=vmem << 20),
            cost_estimate=pl.CostEstimate(flops=flops, bytes_accessed=moved, transcendentals=0),
            interpret=INTERPRET,
            name=name,
        )(*args)

    return run


def silu(v):
    return v / (1.0 + jnp.exp(-v))


def gather_body(ids, x0, y1, y2, y3, c0, c1, c2, c3, piece):
    y, core = ids[3], ids[4]
    for s, (same, other) in enumerate(((x0, c0), (y1, c1), (y2, c2), (y3, c3))):
        chunk = 2 * lax.rem(y + 4 - s, 4)
        piece[pl.ds(pl.multiple_of((chunk + core) * 32, 32), 32), :] = same[...]
        piece[pl.ds(pl.multiple_of((chunk + 1 - core) * 32, 32), 32), :] = other[...]


def project_body(
    ids, x0, y1, y2, y3, c0, c1, c2, c3, w_qk, w_v, piece, pre, tail
):
    gather_body(ids, x0, y1, y2, y3, c0, c1, c2, c3, piece)
    x = piece[...]
    for col, w in ((0, w_qk[0]), (256, w_qk[1]), (512, w_v[:, :256]), (768, w_v[:, 256:])):
        out = jnp.dot(x, w, preferred_element_type=f32).astype(bf16)
        pre[:, col : col + 256] = out
        tail[:, col : col + 256] = out[T - 16 :]


def gate_body(piece, w_g, gain, gate):
    x = piece[...]
    for col in (0, 256):
        lin = jnp.dot(x, w_g[:, col : col + 256], preferred_element_type=f32)
        act = silu(lin)
        for k in (0, 128):
            gate[:, col + k : col + k + 128] = act[:, k : k + 128] * gain[...]


def decay_of(gam_col, gam_row, within):
    return jnp.exp(jnp.where(within, gam_col - gam_row, -1e30))


def masks_of(seg_col, seg_row):
    rows = lax.broadcasted_iota(jnp.int32, (T, T), 0)
    cols = lax.broadcasted_iota(jnp.int32, (T, T), 1)
    return rows, cols, jnp.logical_and(rows >= cols, seg_col == seg_row)


def put_map(ref, both, scale):
    ref[0:128, :] = both.astype(bf16)
    hi = scale.astype(bf16).astype(f32)
    mid = (scale - hi).astype(bf16).astype(f32)
    low = scale - hi - mid
    row = lax.broadcasted_iota(jnp.int32, (16, 256), 0)
    ref[128:144, :] = jnp.where(
        row == 0, hi, jnp.where(row == 1, mid, jnp.where(row == 2, low, 0.0))
    ).astype(bf16)


def get_map(ref):
    both = ref[0:128, :].astype(f32)
    scale = jnp.sum(ref[128:144, 0:1].astype(f32), axis=0, keepdims=True)
    return both, scale


def compose(earlier, later):
    both1, scale1 = earlier
    both2, scale2 = later
    cross = mm(both2[:, 128:], both1)
    b = scale2 * both1[:, :128] + both2[:, :128] - cross[:, :128]
    n = scale2 * both1[:, 128:] + scale1 * both2[:, 128:] - cross[:, 128:]
    return jnp.concatenate([b, n], axis=1), scale1 * scale2


def apply_map(both, scale, state):
    return scale * state - mm(both[:, 128:], state) + both[:, :128]


def recur_body(
    ids, pre, tail, taps, ld, ld_t, beta_t, seg_c, seg_r,
    m0, m1, m2, m3, q_out, kt_out, w_out, gam_c, gam_r, lead_out,
    ext, maps,
):
    first = ids[5]
    x_id = ids[1]
    rows, cols, within = masks_of(seg_c[...], seg_r[...])
    lower = (rows >= cols).astype(f32)
    gam_col = mm_exact(lower, jnp.maximum(ld_t[...], -120.0))
    gam_row = mm_exact(jnp.maximum(ld[...], -120.0), (rows <= cols).astype(f32))
    gam_c[...] = gam_col
    gam_r[...] = gam_row
    lead = jnp.exp(gam_col) * (seg_c[...] < first).astype(f32)
    lead_out[...] = lead

    ext[0:8, :] = tail[8:16, :].astype(f32)
    ext[8 : 8 + T, :] = pre[...].astype(f32)
    position = first + lax.broadcasted_iota(jnp.int32, (T, 1), 0)
    valid = [
        jnp.broadcast_to((position - (CONV - 1) + j >= seg_c[...]).astype(f32), (T, 128))
        for j in range(CONV)
    ]

    def conv(col):
        total = jnp.zeros((T, 128), f32)
        for j in range(CONV):
            total = total + ext[5 + j : 5 + j + T, col : col + 128] * taps[j : j + 1, col : col + 128] * valid[j]
        return silu(total)

    def unit(v):
        return v * lax.rsqrt(jnp.sum(v * v, axis=1, keepdims=True) + 1e-06)

    keys, keys_t, grams = [], [], []
    for g in range(2):
        q_out[:, 128 * g : 128 * g + 128] = (unit(conv(128 * g)) * DK ** (-0.5)).astype(bf16)
        key = unit(conv(256 + 128 * g))
        key_t = key.T.astype(bf16)
        kt_out[g] = key_t
        keys.append(key)
        keys_t.append(key_t)
        grams.append(mm(key, key_t))

    r1 = lax.broadcasted_iota(jnp.int32, (HALF, HALF), 0)
    c1 = lax.broadcasted_iota(jnp.int32, (HALF, HALF), 1)
    gap = jnp.bitwise_xor(r1, c1)
    low = r1 > c1
    unit_mat = (r1 == c1).astype(f32)
    strict = jnp.logical_and(within, rows > cols)
    mats, decays_last = [], []
    for h in range(4):
        gc, gr = gam_col[:, h : h + 1], gam_row[h : h + 1, :]
        a = beta_t[:, h : h + 1] * grams[h // 2] * decay_of(gc, gr, strict)
        mats.append(a)
    blocks = [mats[h][i : i + HALF, i : i + HALF] for h in range(4) for i in (0, HALF)]
    inverse = [unit_mat - jnp.where(jnp.logical_and(low, gap == 1), a, 0.0) for a in blocks]
    size = 2
    while size < HALF:
        at = jnp.logical_and(low, jnp.logical_and(gap >= size, gap < 2 * size))
        left = [mm(x, jnp.where(at, a, 0.0)) for x, a in zip(inverse, blocks)]
        inverse = [x - mm(y, x) for x, y in zip(inverse, left)]
        size *= 2
    last_seg = seg_c[T - 1 : T, :]
    for h in range(4):
        value = conv(512 + 128 * h)
        bet = beta_t[:, h : h + 1]
        rhs = jnp.concatenate(
            [bet * value, (bet * lead[:, h : h + 1]) * keys[h // 2]], axis=1
        )
        top = mm(inverse[2 * h], rhs[:HALF])
        low_rhs = rhs[HALF:] - mm(mats[h][HALF:, :HALF], top)
        bottom = mm(inverse[2 * h + 1], low_rhs)
        w = jnp.concatenate([top, bottom], axis=0)
        w_out[h] = w.astype(bf16)
        gc = gam_col[:, h : h + 1]
        to_end = jnp.exp(
            jnp.where(seg_c[...] == last_seg, gam_col[T - 1 : T, h : h + 1] - gc, -1e30)
        )
        both = mm(keys_t[h // 2], w * to_end)
        put_map(maps.at[h], both, lead[T - 1 : T, h : h + 1])
    for s, out in enumerate((m0, m1, m2, m3)):
        out[...] = maps[lax.rem(x_id + s, 4)]


def local_body(q, k_t, w, gam_c, gam_r, lead, seg_c, seg_r, local, edge):
    _, _, within = masks_of(seg_c[...], seg_r[...])
    for g in range(2):
        query = q[:, 128 * g : 128 * g + 128]
        dots = jnp.dot(query, k_t[g], preferred_element_type=f32)
        for h in (2 * g, 2 * g + 1):
            p = dots * decay_of(gam_c[:, h : h + 1], gam_r[h : h + 1, :], within)
            both = jnp.dot(p.astype(bf16), w[h], preferred_element_type=f32)
            cols = slice(128 * h, 128 * h + 128)
            local[:, cols] = both[:, :128]
            edge[:, cols] = (lead[:, h : h + 1] * query.astype(f32) - both[:, 128:]).astype(bf16)


def group_body(ids, p0, p1, p2, p3, total, before, slots):
    x = ids[1]
    for s, p in enumerate((p0, p1, p2, p3)):
        slots[s] = p[...]
    acc = get_map(slots.at[lax.rem(x + 4, 4)])
    put_map(before.at[0], *acc)
    for j in range(1, 4):
        acc = compose(acc, get_map(slots.at[lax.rem(x + 4 - j, 4)]))
        put_map(before.at[j] if j < 3 else total, *acc)


def depth_body(ids, p0, p1, p2, p3, before, start, whole, slots):
    z = ids[2]
    for s, p in enumerate((p0, p1, p2, p3)):
        slots[s] = p[...]
    acc = get_map(slots.at[z])
    zero = jnp.zeros((128, 256), f32)
    both = jnp.where(z > 0, acc[0], zero)
    scale = jnp.where(z > 0, acc[1], jnp.ones((1, 1), f32))
    for j in range(1, 4):
        acc = compose(acc, get_map(slots.at[lax.rem(z + 4 - j, 4)]))
        if j < 3:
            both = jnp.where(z > j, acc[0], both)
            scale = jnp.where(z > j, acc[1], scale)
    whole[...] = acc[0][:, :128].astype(bf16)
    put_map(start.at[0], both, scale)
    for j in range(3):
        put_map(start.at[j + 1], *compose((both, scale), get_map(before.at[j])))


def spread_body(ids, state, start, s0, s1, s2, s3, slots):
    x = ids[1]
    incoming = state[...].astype(f32)
    for j in range(4):
        slots[j] = apply_map(*get_map(start.at[j]), incoming).astype(bf16)
    for s, out in enumerate((s0, s1, s2, s3)):
        out[...] = slots[lax.rem(x + s, 4)]


def output_body(ids, s0, s1, s2, s3, local, edge, gate, w_o, mine, his, slots, normed):
    x, core = ids[1], ids[4]
    for s, p in enumerate((s0, s1, s2, s3)):
        slots[s] = p[...]
    for h in range(4):
        cols = slice(128 * h, 128 * h + 128)
        state = slots[lax.rem(x + 4 - h, 4)]
        out = local[:, cols] + jnp.dot(edge[:, cols], state, preferred_element_type=f32)
        scale = lax.rsqrt(jnp.mean(out * out, axis=1, keepdims=True) + 1e-06)
        normed[:, cols] = (out * scale * gate[:, cols]).astype(bf16)
    for y in range(4):
        mine[32 * y : 32 * y + 32, :] = normed[pl.ds(pl.multiple_of((2 * y + core) * 32, 32), 32), :]
    other = jnp.concatenate(
        [normed[pl.ds(pl.multiple_of((2 * y + 1 - core) * 32, 32), 32), :] for y in range(4)], axis=0
    )
    for col in range(0, 2048, 256):
        his[:, col : col + 256] = jnp.dot(
            other, w_o[:, col : col + 256], preferred_element_type=f32
        ).astype(bf16)


def mine_body(normed, w_o, out):
    x = normed[...]
    for col in range(0, 2048, 256):
        out[:, col : col + 256] = jnp.dot(x, w_o[:, col : col + 256], preferred_element_type=f32)


def pair_body(ids, mine, got, own, o1, o2, o3):
    y = ids[3]

    def summed(d):
        at = pl.ds(pl.multiple_of(lax.rem(y + d, 4) * 32, 32), 32)
        return mine[at, :] + got[at, :].astype(f32)

    own[...] = summed(0)
    for d, out in ((1, o1), (2, o2), (3, o3)):
        out[...] = summed(d).astype(bf16)


def last_body(own, r1, r2, r3, out):
    out[...] = (
        own[...] + r1[...].astype(f32) + r2[...].astype(f32) + r3[...].astype(f32)
    ).astype(bf16)


def along_y(array, s):
    pairs = [(2 * y + k, 2 * ((y + s) % 4) + k) for y in range(4) for k in range(2)]
    return lax.ppermute(array, "tp", pairs)


def across(array):
    return lax.ppermute(array, "tp", [(i, i ^ 1) for i in range(8)])


def along_x(array, s):
    pairs = [(4 * z + x, 4 * z + (x + s) % 4) for z in range(8) for x in range(4)]
    return lax.ppermute(array, "ctx", pairs)


def along_z(array, s):
    pairs = [
        (16 * g + 4 * z + x, 16 * g + 4 * ((z + s) % 4) + x)
        for g in range(2)
        for z in range(4)
        for x in range(4)
    ]
    return lax.ppermute(array, "ctx", pairs)


def mirrored(array):
    pairs = [(4 * z + x, 4 * (7 - z) + x) for z in range(4) for x in range(4)]
    return lax.ppermute(array, "ctx", pairs)


def local(
    tokens, w_query_key, w_value, w_gate_out, conv_query_key, conv_value,
    log_decay, beta, seg_start, norm_gain, w_output,
):
    ctx = lax.axis_index("ctx")
    tp = lax.axis_index("tp")
    ids = jnp.stack(
        [ctx, ctx % 4, (ctx // 4) % 4, tp // 2, tp % 2, ctx * T, ctx // 16, tp]
    ).astype(jnp.int32)
    taps = jnp.concatenate([conv_query_key[0], conv_query_key[1], conv_value], axis=1)
    ld_t, beta_t = log_decay.T, beta.T
    seg_c, seg_r = seg_start.reshape(T, 1), seg_start.reshape(1, T)
    gain = norm_gain.reshape(1, 128)

    same = [tokens] + [along_y(tokens, s) for s in (1, 2, 3)]
    other = [across(c) for c in same]
    piece, pre, tail = call(
        project_body,
        [((T, 2048), bf16), ((T, 1024), bf16), ((16, 1024), bf16)],
        smem=1, flops=2 * T * 2048 * 1024, name="project",
    )(ids, *same, *other, w_query_key, w_value)
    tail = lax.ppermute(tail, "ctx", [(i, i + 1) for i in range(31)])
    (gate,) = call(gate_body, [((T, 512), f32)], flops=2 * T * 2048 * 512, name="gate")(
        piece, w_gate_out, gain
    )

    pack = ((PACK, 256), bf16)
    *maps, query, key_t, w, gam_c, gam_r, lead = call(
        recur_body,
        [
            pack, pack, pack, pack, ((T, 256), bf16), ((2, 128, T), bf16), ((4, T, 256), bf16),
            ((T, 4), f32), ((4, T), f32), ((T, 4), f32),
        ],
        scratch=[pltpu.VMEM((T + 8, 1024), f32), pltpu.VMEM((4, PACK, 256), bf16)],
        smem=1, flops=10**9, name="recur",
    )(ids, pre, tail, taps, log_decay, ld_t, beta_t, seg_c, seg_r)
    local_out, edge = call(
        local_body, [((T, 512), f32), ((T, 512), bf16)], flops=2 * 10**8, name="local"
    )(query, key_t, w, gam_c, gam_r, lead, seg_c, seg_r)

    slots = [pltpu.VMEM((4, PACK, 256), bf16)]
    maps = [maps[0]] + [along_x(maps[s], s) for s in (1, 2, 3)]
    total, before = call(
        group_body, [pack, ((3, PACK, 256), bf16)], scratch=slots, smem=1, name="group"
    )(ids, *maps)
    totals = [total] + [along_z(total, s) for s in (1, 2, 3)]
    start, whole = call(
        depth_body, [((4, PACK, 256), bf16), ((128, 128), bf16)], scratch=slots, smem=1, name="depth"
    )(ids, *totals, before)
    state = mirrored(whole)
    state_shape = ((128, 128), bf16)
    states = call(
        spread_body, [state_shape] * 4, scratch=[pltpu.VMEM((4, 128, 128), bf16)], smem=1, name="spread"
    )(ids, state, start)
    states = [states[0]] + [along_x(states[s], s) for s in (1, 2, 3)]

    normed, his = call(
        output_body,
        [((HALF, 512), bf16), ((HALF, 2048), bf16)],
        scratch=[pltpu.VMEM((4, 128, 128), bf16), pltpu.VMEM((T, 512), bf16)],
        smem=1, flops=2 * HALF * 512 * 2048, name="output",
    )(ids, *states, local_out, edge, gate, w_output)
    got = across(his)
    (mine,) = call(mine_body, [((HALF, 2048), f32)], flops=2 * HALF * 512 * 2048, name="mine")(
        normed, w_output
    )
    part = ((32, 2048), bf16)
    own, *parts = call(pair_body, [((32, 2048), f32), part, part, part], smem=1, name="pair")(
        ids, mine, got
    )
    parts = [along_y(parts[s - 1], s) for s in (1, 2, 3)]
    return call(last_body, [part], name="last")(own, *parts)[0]


def solution(mesh):
    return jax.shard_map(
        local,
        mesh=mesh,
        in_specs=(
            P(("ctx", "tp"), None),
            P(None, None, "tp"),
            P(None, "tp"),
            P(None, "tp"),
            P(None, None, "tp"),
            P(None, "tp"),
            P("tp", "ctx"),
            P("tp", "ctx"),
            P("ctx"),
            P(),
            P("tp", None),
        ),
        out_specs=P(("ctx", "tp"), None),
        check_vma=False,
    )
```

```python
import functools

import jax
import jax.numpy as jnp
from jax import lax
from jax.experimental import pallas as pl
from jax.experimental.pallas import tpu as pltpu
from jax.sharding import PartitionSpec as P


DK = 128
CONV = 4
T = 256
HALF = 128
PACK = 144
f32 = jnp.float32
bf16 = jnp.bfloat16
INTERPRET = False


def mm(a, b):
    return jnp.dot(a.astype(bf16), b.astype(bf16), preferred_element_type=f32)


def mm_exact(a, b):
    return jnp.dot(a, b, preferred_element_type=f32, precision=lax.Precision.HIGHEST)


def call(kernel, outs, scratch=(), smem=0, far=0, vmem=16, flops=0, name=None):
    def run(*args):
        args = [
            pltpu.with_memory_space_constraint(a, pltpu.HBM) if smem <= i < smem + far and not INTERPRET else a
            for i, a in enumerate(args)
        ]
        spaces = [pltpu.SMEM] * smem + [pltpu.HBM] * far + [pltpu.VMEM] * (len(args) - smem - far)
        in_specs = [pl.BlockSpec(memory_space=space) for space in spaces]
        shapes = [jax.ShapeDtypeStruct(s, d) for s, d in outs]
        moved = sum(a.size * a.dtype.itemsize for a in args) + sum(
            s.size * s.dtype.itemsize for s in shapes
        )
        return pl.pallas_call(
            kernel,
            out_shape=shapes,
            in_specs=in_specs,
            out_specs=[pl.BlockSpec(memory_space=pltpu.VMEM)] * len(outs),
            scratch_shapes=list(scratch),
            compiler_params=pltpu.CompilerParams(vmem_limit_bytes=vmem << 20),
            cost_estimate=pl.CostEstimate(flops=flops, bytes_accessed=moved, transcendentals=0),
            interpret=INTERPRET,
            name=name,
        )(*args)

    return run


def silu(v):
    return v / (1.0 + jnp.exp(-v))


def prepare_body(
    ids, ld_far, beta_far, seg_far, w_qk, w_v, w_g, w_o,
    w_qk_near, w_v_near, w_g_near, w_o_near, cols_out, decay_out, ld, beta, seg_r, sems,
):
    pairs = (
        (ld_far, ld), (beta_far, beta), (seg_far, seg_r),
        (w_qk, w_qk_near), (w_v, w_v_near), (w_g, w_g_near), (w_o, w_o_near),
    )
    copies = [pltpu.make_async_copy(src, dst, sems.at[i]) for i, (src, dst) in enumerate(pairs)]
    for copy in copies:
        copy.start()
    for copy in copies[:3]:
        copy.wait()
    first = ids[5].astype(f32)
    seg_row = seg_r[...].astype(f32)
    clipped = jnp.maximum(ld[...], -120.0)
    rows = lax.broadcasted_iota(jnp.int32, (T, T), 0)
    cols = lax.broadcasted_iota(jnp.int32, (T, T), 1)
    gam_row = mm_exact(
        jnp.concatenate([clipped, jnp.zeros((4, T), f32)], axis=0), (rows <= cols).astype(f32)
    )
    gam_col = gam_row.T[:, :4]
    columns = jnp.concatenate([beta[...], jnp.broadcast_to(seg_row, (4, T))], axis=0).T
    beta_col, seg_col = columns[:, :4], columns[:, 4:5]
    lead = jnp.exp(gam_col) * (seg_col < first).astype(f32)
    same_end = seg_col == seg_row[:, T - 1 :]
    to_end = jnp.exp(jnp.where(same_end, gam_col[T - 1 :] - gam_col, -1e30))
    cols_out[...] = jnp.concatenate([beta_col, lead, to_end, jnp.broadcast_to(seg_col, (T, 4))], axis=1)
    within = jnp.logical_and(rows >= cols, seg_col == seg_row)
    for h in range(4):
        decay_out[h] = jnp.exp(jnp.where(within, gam_col[:, h : h + 1] - gam_row[h : h + 1], -1e30))
    for copy in copies[3:]:
        copy.wait()


def gather_body(ids, x0, y1, y2, y3, c0, c1, c2, c3, piece):
    y, core = ids[3], ids[4]
    for s, (same, other) in enumerate(((x0, c0), (y1, c1), (y2, c2), (y3, c3))):
        chunk = 2 * jnp.bitwise_xor(y, s)
        piece[pl.ds(pl.multiple_of((chunk + core) * 32, 32), 32), :] = same[...]
        piece[pl.ds(pl.multiple_of((chunk + 1 - core) * 32, 32), 32), :] = other[...]


def project_body(
    ids, x0, y1, y2, y3, c0, c1, c2, c3, w_qk, w_v, piece, pre, tail
):
    gather_body(ids, x0, y1, y2, y3, c0, c1, c2, c3, piece)
    x = piece[...]
    for col, w in ((0, w_qk[0]), (256, w_qk[1]), (512, w_v[:, :256]), (768, w_v[:, 256:])):
        out = jnp.dot(x, w, preferred_element_type=f32).astype(bf16)
        pre[:, col : col + 256] = out
        tail[:, col : col + 256] = out[T - 16 :]


def gate_body(piece, w_g, gain, gate):
    x = piece[...]
    for col in (0, 256):
        lin = jnp.dot(x, w_g[:, col : col + 256], preferred_element_type=f32)
        act = silu(lin)
        for k in (0, 128):
            gate[:, col + k : col + k + 128] = act[:, k : k + 128] * gain[...]


def put_map(ref, both, scale):
    ref[0:128, :] = both.astype(bf16)
    hi = scale.astype(bf16).astype(f32)
    mid = (scale - hi).astype(bf16).astype(f32)
    low = scale - hi - mid
    row = lax.broadcasted_iota(jnp.int32, (16, 256), 0)
    ref[128:144, :] = jnp.where(
        row == 0, hi, jnp.where(row == 1, mid, jnp.where(row == 2, low, 0.0))
    ).astype(bf16)


def get_map(ref):
    both = ref[0:128, :].astype(f32)
    scale = jnp.sum(ref[128:144, 0:1].astype(f32), axis=0, keepdims=True)
    return both, scale


def compose(earlier, later):
    both1, scale1 = earlier
    both2, scale2 = later
    cross = mm(both2[:, 128:], both1)
    b = scale2 * both1[:, :128] + both2[:, :128] - cross[:, :128]
    n = scale2 * both1[:, 128:] + scale1 * both2[:, 128:] - cross[:, 128:]
    return jnp.concatenate([b, n], axis=1), scale1 * scale2


def apply_map(both, scale, state):
    return scale * state - mm(both[:, 128:], state) + both[:, :128]


def recur_body(
    ids, pre, tail, taps_qk, taps_v, columns, decay,
    m0, m1, m2, m3, q_out, kt_out, w_out,
    ext, maps,
):
    first = ids[5]
    x_id = ids[1]
    ext[0:8, :] = tail[8:16, :].astype(f32)
    ext[8 : 8 + T, :] = pre[...].astype(f32)
    age = (first + lax.broadcasted_iota(jnp.int32, (T, 1), 0)).astype(f32) - columns[:, 12:13]
    valid = [
        jnp.broadcast_to((age >= CONV - 1 - j).astype(f32), (T, 128)) for j in range(CONV)
    ]

    def conv(col, taps):
        total = ext[8 : 8 + T, col : col + 128] * taps[CONV - 1 : CONV]
        for j in range(CONV - 1):
            total = total + ext[5 + j : 5 + j + T, col : col + 128] * taps[j : j + 1] * valid[j]
        return silu(total)

    def unit(v):
        return v * lax.rsqrt(jnp.sum(v * v, axis=1, keepdims=True) + 1e-06)

    keys, keys_t, grams = [], [], []
    for g in range(2):
        q_out[:, 128 * g : 128 * g + 128] = (unit(conv(128 * g, taps_qk[0, :, 128 * g : 128 * g + 128])) * DK ** (-0.5)).astype(bf16)
        key = unit(conv(256 + 128 * g, taps_qk[1, :, 128 * g : 128 * g + 128]))
        key_t = key.T.astype(bf16)
        kt_out[g] = key_t
        keys.append(key)
        keys_t.append(key_t)
        grams.append(mm(key, key_t))

    r1 = lax.broadcasted_iota(jnp.int32, (HALF, HALF), 0)
    c1 = lax.broadcasted_iota(jnp.int32, (HALF, HALF), 1)
    gap = jnp.bitwise_xor(r1, c1)
    low = r1 > c1
    unit_mat = (r1 == c1).astype(f32)
    mats = [columns[:, h : h + 1] * grams[h // 2] * decay[h] for h in range(4)]
    blocks = [mats[h][i : i + HALF, i : i + HALF] for h in range(4) for i in (0, HALF)]
    inverse = [unit_mat - jnp.where(jnp.logical_and(low, gap == 1), a, 0.0) for a in blocks]
    size = 2
    while size < HALF:
        at = jnp.logical_and(low, jnp.logical_and(gap >= size, gap < 2 * size))
        left = [mm(x, jnp.where(at, a, 0.0)) for x, a in zip(inverse, blocks)]
        inverse = [x - mm(y, x) for x, y in zip(inverse, left)]
        size *= 2
    for h in range(4):
        value = conv(512 + 128 * h, taps_v[:, 128 * h : 128 * h + 128])
        bet = columns[:, h : h + 1]
        lead = columns[:, 4 + h : 5 + h]
        rhs = jnp.concatenate(
            [bet * value, (bet * lead) * keys[h // 2]], axis=1
        )
        top = mm(inverse[2 * h], rhs[:HALF])
        low_rhs = rhs[HALF:] - mm(mats[h][HALF:, :HALF], top)
        bottom = mm(inverse[2 * h + 1], low_rhs)
        w = jnp.concatenate([top, bottom], axis=0)
        w_out[h] = w.astype(bf16)
        both = mm(keys_t[h // 2], w * columns[:, 8 + h : 9 + h])
        put_map(maps.at[h], both, lead[T - 1 : T])
    for s, out in enumerate((m0, m1, m2, m3)):
        out[...] = maps[jnp.bitwise_xor(x_id, s)]


def local_body(q, k_t, w, columns, decay, local, edge):
    for g in range(2):
        query = q[:, 128 * g : 128 * g + 128]
        dots = jnp.dot(query, k_t[g], preferred_element_type=f32)
        for h in (2 * g, 2 * g + 1):
            p = dots * decay[h]
            both = jnp.dot(p.astype(bf16), w[h], preferred_element_type=f32)
            cols = slice(128 * h, 128 * h + 128)
            local[:, cols] = both[:, :128]
            edge[:, cols] = (columns[:, 4 + h : 5 + h] * query.astype(f32) - both[:, 128:]).astype(bf16)


def group_body(ids, p0, p1, p2, p3, total, before, slots):
    x = ids[1]
    for s, p in enumerate((p0, p1, p2, p3)):
        slots[s] = p[...]
    acc = get_map(slots.at[x])
    put_map(before.at[0], *acc)
    for j in range(1, 4):
        acc = compose(acc, get_map(slots.at[jnp.bitwise_xor(x, j)]))
        put_map(before.at[j] if j < 3 else total, *acc)


def depth_body(ids, p0, p1, p2, p3, before, start, whole, slots):
    z = ids[2]
    for s, p in enumerate((p0, p1, p2, p3)):
        slots[s] = p[...]
    acc = get_map(slots.at[z])
    zero = jnp.zeros((128, 256), f32)
    both = jnp.where(z > 0, acc[0], zero)
    scale = jnp.where(z > 0, acc[1], jnp.ones((1, 1), f32))
    for j in range(1, 4):
        acc = compose(acc, get_map(slots.at[jnp.bitwise_xor(z, j)]))
        if j < 3:
            both = jnp.where(z > j, acc[0], both)
            scale = jnp.where(z > j, acc[1], scale)
    whole[...] = acc[0][:, :128].astype(bf16)
    put_map(start.at[0], both, scale)
    for j in range(3):
        put_map(start.at[j + 1], *compose((both, scale), get_map(before.at[j])))


def spread_body(ids, state, start, s0, s1, s2, s3, slots):
    x = ids[1]
    incoming = jnp.where(ids[6] > 0, state[...].astype(f32), 0.0)
    for j in range(4):
        slots[j] = apply_map(*get_map(start.at[j]), incoming).astype(bf16)
    for s, out in enumerate((s0, s1, s2, s3)):
        out[...] = slots[jnp.bitwise_xor(x, s)]


def output_body(ids, s0, s1, s2, s3, local, edge, gate, w_o, mine, his, slots, normed):
    x, core = ids[1], ids[4]
    for s, p in enumerate((s0, s1, s2, s3)):
        slots[s] = p[...]
    for h in range(4):
        cols = slice(128 * h, 128 * h + 128)
        state = slots[jnp.bitwise_xor(x, h)]
        out = local[:, cols] + jnp.dot(edge[:, cols], state, preferred_element_type=f32)
        scale = lax.rsqrt(jnp.mean(out * out, axis=1, keepdims=True) + 1e-06)
        normed[:, cols] = (out * scale * gate[:, cols]).astype(bf16)
    for y in range(4):
        mine[32 * y : 32 * y + 32, :] = normed[pl.ds(pl.multiple_of((2 * y + core) * 32, 32), 32), :]
    other = jnp.concatenate(
        [normed[pl.ds(pl.multiple_of((2 * y + 1 - core) * 32, 32), 32), :] for y in range(4)], axis=0
    )
    for col in range(0, 2048, 256):
        his[:, col : col + 256] = jnp.dot(
            other, w_o[:, col : col + 256], preferred_element_type=f32
        ).astype(bf16)


def mine_body(normed, w_o, out):
    x = normed[...]
    for col in range(0, 2048, 256):
        out[:, col : col + 256] = jnp.dot(x, w_o[:, col : col + 256], preferred_element_type=f32)


def pair_body(ids, mine, got, own, o1, o2, o3):
    y = ids[3]

    def summed(d):
        at = pl.ds(pl.multiple_of(jnp.bitwise_xor(y, d) * 32, 32), 32)
        return mine[at, :] + got[at, :].astype(f32)

    own[...] = summed(0)
    for d, out in ((1, o1), (2, o2), (3, o3)):
        out[...] = summed(d).astype(bf16)


def last_body(own, r1, r2, r3, out):
    out[...] = (
        own[...] + r1[...].astype(f32) + r2[...].astype(f32) + r3[...].astype(f32)
    ).astype(bf16)


def along_y(array, s):
    pairs = [(2 * y + k, 2 * (y ^ s) + k) for y in range(4) for k in range(2)]
    return lax.ppermute(array, "tp", pairs)


def across(array):
    return lax.ppermute(array, "tp", [(i, i ^ 1) for i in range(8)])


def along_x(array, s):
    pairs = [(4 * z + x, 4 * z + (x ^ s)) for z in range(8) for x in range(4)]
    return lax.ppermute(array, "ctx", pairs)


def along_z(array, s):
    pairs = [
        (16 * g + 4 * z + x, 16 * g + 4 * (z ^ s) + x)
        for g in range(2)
        for z in range(4)
        for x in range(4)
    ]
    return lax.ppermute(array, "ctx", pairs)


def mirrored(array):
    pairs = [(4 * z + x, 4 * (7 - z) + x) for z in range(8) for x in range(4)]
    return lax.ppermute(array, "ctx", pairs)


def local(
    tokens, w_query_key, w_value, w_gate_out, conv_query_key, conv_value,
    log_decay, beta, seg_start, norm_gain, w_output,
):
    ctx = lax.axis_index("ctx")
    tp = lax.axis_index("tp")
    ids = jnp.stack(
        [ctx, ctx % 4, (ctx // 4) % 4, tp // 2, tp % 2, ctx * T, ctx // 16, tp]
    ).astype(jnp.int32)
    seg_r = seg_start.reshape(1, T)
    gain = norm_gain.reshape(1, 128)
    near = lambda a: (a.shape, a.dtype)

    same = [tokens] + [along_y(tokens, s) for s in (2, 1, 3)]
    same = [same[0], same[2], same[1], same[3]]
    weights = (w_query_key, w_value, w_gate_out, w_output)
    w_query_key, w_value, w_gate_out, w_output, columns, decay = call(
        prepare_body,
        [near(w) for w in weights] + [((T, 16), f32), ((4, T, T), f32)],
        scratch=[
            pltpu.VMEM((4, T), f32), pltpu.VMEM((4, T), f32), pltpu.VMEM((1, T), jnp.int32),
            pltpu.SemaphoreType.DMA((7,)),
        ],
        smem=1, far=7, flops=10**8, name="prepare",
    )(ids, log_decay, beta, seg_r, *weights)
    other = [across(lax.optimization_barrier((c, columns))[0]) for c in same]
    piece, pre, tail = call(
        project_body,
        [((T, 2048), bf16), ((T, 1024), bf16), ((16, 1024), bf16)],
        smem=1, flops=2 * T * 2048 * 1024, name="project",
    )(ids, *same, *other, w_query_key, w_value)
    tail = lax.ppermute(tail, "ctx", [(i, i + 1) for i in range(31)])
    (gate,) = call(gate_body, [((T, 512), f32)], flops=2 * T * 2048 * 512, name="gate")(
        piece, w_gate_out, gain
    )

    pack = ((PACK, 256), bf16)
    *maps, query, key_t, w = call(
        recur_body,
        [pack, pack, pack, pack, ((T, 256), bf16), ((2, 128, T), bf16), ((4, T, 256), bf16)],
        scratch=[pltpu.VMEM((T + 8, 1024), f32), pltpu.VMEM((4, PACK, 256), bf16)],
        smem=1, flops=10**9, name="recur",
    )(ids, pre, tail, conv_query_key, conv_value, columns, decay)
    local_out, edge = call(
        local_body, [((T, 512), f32), ((T, 512), bf16)], flops=2 * 10**8, name="local"
    )(query, key_t, w, columns, decay)

    slots = [pltpu.VMEM((4, PACK, 256), bf16)]
    maps = [maps[0]] + [along_x(maps[s], s) for s in (1, 2, 3)]
    total, before = call(
        group_body, [pack, ((3, PACK, 256), bf16)], scratch=slots, smem=1, name="group"
    )(ids, *maps)
    totals = [total] + [along_z(total, s) for s in (1, 2, 3)]
    start, whole = call(
        depth_body, [((4, PACK, 256), bf16), ((128, 128), bf16)], scratch=slots, smem=1, name="depth"
    )(ids, *totals, before)
    state_shape = ((128, 128), bf16)
    states = call(
        spread_body, [state_shape] * 4, scratch=[pltpu.VMEM((4, 128, 128), bf16)], smem=1, name="spread"
    )(ids, mirrored(whole), start)
    states = [states[0]] + [along_x(states[s], s) for s in (1, 2, 3)]

    normed, his = call(
        output_body,
        [((HALF, 512), bf16), ((HALF, 2048), bf16)],
        scratch=[pltpu.VMEM((4, 128, 128), bf16), pltpu.VMEM((T, 512), bf16)],
        smem=1, flops=2 * HALF * 512 * 2048, name="output",
    )(ids, *states, local_out, edge, gate, w_output)
    got = across(his)
    (mine,) = call(mine_body, [((HALF, 2048), f32)], flops=2 * HALF * 512 * 2048, name="mine")(
        normed, w_output
    )
    part = ((32, 2048), bf16)
    own, *parts = call(pair_body, [((32, 2048), f32), part, part, part], smem=1, name="pair")(
        ids, mine, got
    )
    parts = [along_y(parts[s - 1], s) for s in (1, 2, 3)]
    return call(last_body, [part], name="last")(own, *parts)[0]


def solution(mesh):
    return jax.shard_map(
        local,
        mesh=mesh,
        in_specs=(
            P(("ctx", "tp"), None),
            P(None, None, "tp"),
            P(None, "tp"),
            P(None, "tp"),
            P(None, None, "tp"),
            P(None, "tp"),
            P("tp", "ctx"),
            P("tp", "ctx"),
            P("ctx"),
            P(),
            P("tp", None),
        ),
        out_specs=P(("ctx", "tp"), None),
        check_vma=False,
    )
```

```python
import functools

import jax
import jax.numpy as jnp
from jax import lax
from jax.experimental import pallas as pl
from jax.experimental.pallas import tpu as pltpu
from jax.sharding import PartitionSpec as P


DK = 128
CONV = 4
T = 256
HALF = 128
PACK = 144
f32 = jnp.float32
bf16 = jnp.bfloat16
INTERPRET = False


def mm(a, b):
    return jnp.dot(a.astype(bf16), b.astype(bf16), preferred_element_type=f32)


def mm_exact(a, b):
    return jnp.dot(a, b, preferred_element_type=f32, precision=lax.Precision.HIGHEST)


def call(kernel, outs, scratch=(), smem=0, far=0, vmem=16, flops=0, name=None):
    def run(*args):
        args = [
            pltpu.with_memory_space_constraint(a, pltpu.HBM) if smem <= i < smem + far and not INTERPRET else a
            for i, a in enumerate(args)
        ]
        spaces = [pltpu.SMEM] * smem + [pltpu.HBM] * far + [pltpu.VMEM] * (len(args) - smem - far)
        in_specs = [pl.BlockSpec(memory_space=space) for space in spaces]
        shapes = [jax.ShapeDtypeStruct(s, d) for s, d in outs]
        moved = sum(a.size * a.dtype.itemsize for a in args) + sum(
            s.size * s.dtype.itemsize for s in shapes
        )
        return pl.pallas_call(
            kernel,
            out_shape=shapes,
            in_specs=in_specs,
            out_specs=[pl.BlockSpec(memory_space=pltpu.VMEM)] * len(outs),
            scratch_shapes=list(scratch),
            compiler_params=pltpu.CompilerParams(vmem_limit_bytes=vmem << 20),
            cost_estimate=pl.CostEstimate(flops=flops, bytes_accessed=moved, transcendentals=0),
            interpret=INTERPRET,
            name=name,
        )(*args)

    return run


def silu(v):
    return v / (1.0 + jnp.exp(-v))


def prepare_body(
    ids, ld_far, beta_far, seg_far, w_qk, w_v, w_g, w_o,
    w_qk_near, w_v_near, w_g_near, w_o_near, cols_out, decay_out, ld, beta, seg_r, sems,
):
    pairs = (
        (ld_far, ld), (beta_far, beta), (seg_far, seg_r),
        (w_qk, w_qk_near), (w_v, w_v_near), (w_g, w_g_near), (w_o, w_o_near),
    )
    copies = [pltpu.make_async_copy(src, dst, sems.at[i]) for i, (src, dst) in enumerate(pairs)]
    for copy in copies:
        copy.start()
    for copy in copies[:3]:
        copy.wait()
    first = ids[5].astype(f32)
    seg_row = seg_r[...].astype(f32)
    clipped = jnp.maximum(ld[...], -120.0)
    rows = lax.broadcasted_iota(jnp.int32, (T, T), 0)
    cols = lax.broadcasted_iota(jnp.int32, (T, T), 1)
    gam_row = mm_exact(
        jnp.concatenate([clipped, jnp.zeros((4, T), f32)], axis=0), (rows <= cols).astype(f32)
    )
    gam_col = gam_row.T[:, :4]
    columns = jnp.concatenate([beta[...], jnp.broadcast_to(seg_row, (4, T))], axis=0).T
    beta_col, seg_col = columns[:, :4], columns[:, 4:5]
    lead = jnp.exp(gam_col) * (seg_col < first).astype(f32)
    same_end = seg_col == seg_row[:, T - 1 :]
    to_end = jnp.exp(jnp.where(same_end, gam_col[T - 1 :] - gam_col, -1e30))
    cols_out[...] = jnp.concatenate([beta_col, lead, to_end, jnp.broadcast_to(seg_col, (T, 4))], axis=1)
    within = jnp.logical_and(rows >= cols, seg_col == seg_row)
    for h in range(4):
        decay_out[h] = jnp.exp(jnp.where(within, gam_col[:, h : h + 1] - gam_row[h : h + 1], -1e30))
    for copy in copies[3:]:
        copy.wait()


def gather_body(ids, x0, c0, same, other, piece):
    y, core = ids[3], ids[4]
    for s in range(4):
        chunk = 2 * lax.rem(y + 4 - s, 4)
        rows = slice(32 * s - 32, 32 * s)
        near = same[rows, :] if s else x0[...]
        far = other[rows, :] if s else c0[...]
        piece[pl.ds(pl.multiple_of((chunk + core) * 32, 32), 32), :] = near
        piece[pl.ds(pl.multiple_of((chunk + 1 - core) * 32, 32), 32), :] = far


def project_body(
    ids, x0, c0, same, other, w_qk, w_v, piece, pre, tail
):
    gather_body(ids, x0, c0, same, other, piece)
    x = piece[...]
    for col, w in ((0, w_qk[0]), (256, w_qk[1]), (512, w_v[:, :256]), (768, w_v[:, 256:])):
        out = jnp.dot(x, w, preferred_element_type=f32).astype(bf16)
        pre[:, col : col + 256] = out
        tail[:, col : col + 256] = out[T - 16 :]


def gate_body(piece, w_g, gain, gate):
    x = piece[...]
    for col in (0, 256):
        lin = jnp.dot(x, w_g[:, col : col + 256], preferred_element_type=f32)
        act = silu(lin)
        for k in (0, 128):
            gate[:, col + k : col + k + 128] = act[:, k : k + 128] * gain[...]


def put_map(ref, both, scale):
    ref[0:128, :] = both.astype(bf16)
    hi = scale.astype(bf16).astype(f32)
    mid = (scale - hi).astype(bf16).astype(f32)
    low = scale - hi - mid
    row = lax.broadcasted_iota(jnp.int32, (16, 256), 0)
    ref[128:144, :] = jnp.where(
        row == 0, hi, jnp.where(row == 1, mid, jnp.where(row == 2, low, 0.0))
    ).astype(bf16)


def get_map(ref):
    both = ref[0:128, :].astype(f32)
    scale = jnp.sum(ref[128:144, 0:1].astype(f32), axis=0, keepdims=True)
    return both, scale


def compose(earlier, later):
    both1, scale1 = earlier
    both2, scale2 = later
    cross = mm(both2[:, 128:], both1)
    b = scale2 * both1[:, :128] + both2[:, :128] - cross[:, :128]
    n = scale2 * both1[:, 128:] + scale1 * both2[:, 128:] - cross[:, 128:]
    return jnp.concatenate([b, n], axis=1), scale1 * scale2


def apply_map(both, scale, state):
    return scale * state - mm(both[:, 128:], state) + both[:, :128]


def recur_body(
    ids, pre, tail, taps_qk, taps_v, columns, decay,
    m0, m1, m2, m3, q_out, kt_out, w_out,
    ext, maps,
):
    first = ids[5]
    x_id = ids[1]
    ext[0:8, :] = tail[8:16, :].astype(f32)
    ext[8 : 8 + T, :] = pre[...].astype(f32)
    age = (first + lax.broadcasted_iota(jnp.int32, (T, 1), 0)).astype(f32) - columns[:, 12:13]
    valid = [
        jnp.broadcast_to((age >= CONV - 1 - j).astype(f32), (T, 128)) for j in range(CONV)
    ]

    def conv(col, taps):
        total = ext[8 : 8 + T, col : col + 128] * taps[CONV - 1 : CONV]
        for j in range(CONV - 1):
            total = total + ext[5 + j : 5 + j + T, col : col + 128] * taps[j : j + 1] * valid[j]
        return silu(total)

    def unit(v):
        return v * lax.rsqrt(jnp.sum(v * v, axis=1, keepdims=True) + 1e-06)

    keys, keys_t, grams = [], [], []
    for g in range(2):
        q_out[:, 128 * g : 128 * g + 128] = (unit(conv(128 * g, taps_qk[0, :, 128 * g : 128 * g + 128])) * DK ** (-0.5)).astype(bf16)
        key = unit(conv(256 + 128 * g, taps_qk[1, :, 128 * g : 128 * g + 128]))
        key_t = key.T.astype(bf16)
        kt_out[g] = key_t
        keys.append(key)
        keys_t.append(key_t)
        grams.append(mm(key, key_t))

    r1 = lax.broadcasted_iota(jnp.int32, (HALF, HALF), 0)
    c1 = lax.broadcasted_iota(jnp.int32, (HALF, HALF), 1)
    gap = jnp.bitwise_xor(r1, c1)
    low = r1 > c1
    unit_mat = (r1 == c1).astype(f32)
    mats = [columns[:, h : h + 1] * grams[h // 2] * decay[h] for h in range(4)]
    blocks = [mats[h][i : i + HALF, i : i + HALF] for h in range(4) for i in (0, HALF)]
    inverse = [unit_mat - jnp.where(jnp.logical_and(low, gap == 1), a, 0.0) for a in blocks]
    size = 2
    while size < HALF:
        at = jnp.logical_and(low, jnp.logical_and(gap >= size, gap < 2 * size))
        left = [mm(x, jnp.where(at, a, 0.0)) for x, a in zip(inverse, blocks)]
        inverse = [x - mm(y, x) for x, y in zip(inverse, left)]
        size *= 2
    for h in range(4):
        value = conv(512 + 128 * h, taps_v[:, 128 * h : 128 * h + 128])
        bet = columns[:, h : h + 1]
        lead = columns[:, 4 + h : 5 + h]
        rhs = jnp.concatenate(
            [bet * value, (bet * lead) * keys[h // 2]], axis=1
        )
        top = mm(inverse[2 * h], rhs[:HALF])
        low_rhs = rhs[HALF:] - mm(mats[h][HALF:, :HALF], top)
        bottom = mm(inverse[2 * h + 1], low_rhs)
        w = jnp.concatenate([top, bottom], axis=0)
        w_out[h] = w.astype(bf16)
        both = mm(keys_t[h // 2], w * columns[:, 8 + h : 9 + h])
        put_map(maps.at[h], both, lead[T - 1 : T])
    for s, out in enumerate((m0, m1, m2, m3)):
        out[...] = maps[jnp.bitwise_xor(x_id, s)]


def local_body(q, k_t, w, columns, decay, local, edge):
    for g in range(2):
        query = q[:, 128 * g : 128 * g + 128]
        dots = jnp.dot(query, k_t[g], preferred_element_type=f32)
        for h in (2 * g, 2 * g + 1):
            p = dots * decay[h]
            both = jnp.dot(p.astype(bf16), w[h], preferred_element_type=f32)
            cols = slice(128 * h, 128 * h + 128)
            local[:, cols] = both[:, :128]
            edge[:, cols] = (columns[:, 4 + h : 5 + h] * query.astype(f32) - both[:, 128:]).astype(bf16)


def group_body(ids, p0, p1, p2, p3, total, before, slots):
    x = ids[1]
    for s, p in enumerate((p0, p1, p2, p3)):
        slots[s] = p[...]
    acc = get_map(slots.at[x])
    put_map(before.at[0], *acc)
    for j in range(1, 4):
        acc = compose(acc, get_map(slots.at[jnp.bitwise_xor(x, j)]))
        put_map(before.at[j] if j < 3 else total, *acc)


def depth_body(ids, p0, p1, p2, p3, before, start, whole, slots):
    z = ids[2]
    for s, p in enumerate((p0, p1, p2, p3)):
        slots[s] = p[...]
    acc = get_map(slots.at[z])
    zero = jnp.zeros((128, 256), f32)
    both = jnp.where(z > 0, acc[0], zero)
    scale = jnp.where(z > 0, acc[1], jnp.ones((1, 1), f32))
    for j in range(1, 4):
        acc = compose(acc, get_map(slots.at[jnp.bitwise_xor(z, j)]))
        if j < 3:
            both = jnp.where(z > j, acc[0], both)
            scale = jnp.where(z > j, acc[1], scale)
    whole[...] = acc[0][:, :128].astype(bf16)
    put_map(start.at[0], both, scale)
    for j in range(3):
        put_map(start.at[j + 1], *compose((both, scale), get_map(before.at[j])))


def spread_body(ids, state, start, s0, s1, s2, s3, slots):
    x = ids[1]
    incoming = jnp.where(ids[6] > 0, state[...].astype(f32), 0.0)
    for j in range(4):
        slots[j] = apply_map(*get_map(start.at[j]), incoming).astype(bf16)
    for s, out in enumerate((s0, s1, s2, s3)):
        out[...] = slots[jnp.bitwise_xor(x, s)]


def output_body(ids, s0, s1, s2, s3, local, edge, gate, w_o, mine, his, slots, normed):
    x, core = ids[1], ids[4]
    for s, p in enumerate((s0, s1, s2, s3)):
        slots[s] = p[...]
    for h in range(4):
        cols = slice(128 * h, 128 * h + 128)
        state = slots[jnp.bitwise_xor(x, h)]
        out = local[:, cols] + jnp.dot(edge[:, cols], state, preferred_element_type=f32)
        scale = lax.rsqrt(jnp.mean(out * out, axis=1, keepdims=True) + 1e-06)
        normed[:, cols] = (out * scale * gate[:, cols]).astype(bf16)
    for y in range(4):
        mine[32 * y : 32 * y + 32, :] = normed[pl.ds(pl.multiple_of((2 * y + core) * 32, 32), 32), :]
    other = jnp.concatenate(
        [normed[pl.ds(pl.multiple_of((2 * y + 1 - core) * 32, 32), 32), :] for y in range(4)], axis=0
    )
    for col in range(0, 2048, 256):
        his[:, col : col + 256] = jnp.dot(
            other, w_o[:, col : col + 256], preferred_element_type=f32
        ).astype(bf16)


def mine_body(normed, w_o, out):
    x = normed[...]
    for col in range(0, 2048, 256):
        out[:, col : col + 256] = jnp.dot(x, w_o[:, col : col + 256], preferred_element_type=f32)


def pair_body(ids, mine, got, own, o1, o2, o3):
    y = ids[3]

    def summed(d):
        at = pl.ds(pl.multiple_of(lax.rem(y + d, 4) * 32, 32), 32)
        return mine[at, :] + got[at, :].astype(f32)

    own[...] = summed(0)
    for d, out in ((1, o1), (2, o2), (3, o3)):
        out[...] = summed(d).astype(bf16)


def last_body(own, r1, r2, r3, out):
    out[...] = (
        own[...] + r1[...].astype(f32) + r2[...].astype(f32) + r3[...].astype(f32)
    ).astype(bf16)


def along_y(array, s):
    pairs = [(2 * y + k, 2 * ((y + s) % 4) + k) for y in range(4) for k in range(2)]
    return lax.ppermute(array, "tp", pairs)


def across(array):
    return lax.ppermute(array, "tp", [(i, i ^ 1) for i in range(8)])


def along_x(array, s):
    pairs = [(4 * z + x, 4 * z + (x ^ s)) for z in range(8) for x in range(4)]
    return lax.ppermute(array, "ctx", pairs)


def along_z(array, s):
    pairs = [
        (16 * g + 4 * z + x, 16 * g + 4 * (z ^ s) + x)
        for g in range(2)
        for z in range(4)
        for x in range(4)
    ]
    return lax.ppermute(array, "ctx", pairs)


def mirrored(array):
    pairs = [(4 * z + x, 4 * (7 - z) + x) for z in range(8) for x in range(4)]
    return lax.ppermute(array, "ctx", pairs)


def local(
    tokens, w_query_key, w_value, w_gate_out, conv_query_key, conv_value,
    log_decay, beta, seg_start, norm_gain, w_output,
):
    ctx = lax.axis_index("ctx")
    tp = lax.axis_index("tp")
    ids = jnp.stack(
        [ctx, ctx % 4, (ctx // 4) % 4, tp // 2, tp % 2, ctx * T, ctx // 16, tp]
    ).astype(jnp.int32)
    seg_r = seg_start.reshape(1, T)
    gain = norm_gain.reshape(1, 128)
    near = lambda a: (a.shape, a.dtype)

    moved = {s: along_y(tokens, s) for s in (2, 1, 3)}
    swapped = across(tokens)
    weights = (w_query_key, w_value, w_gate_out, w_output)
    w_query_key, w_value, w_gate_out, w_output, columns, decay = call(
        prepare_body,
        [near(w) for w in weights] + [((T, 16), f32), ((4, T, T), f32)],
        scratch=[
            pltpu.VMEM((4, T), f32), pltpu.VMEM((4, T), f32), pltpu.VMEM((1, T), jnp.int32),
            pltpu.SemaphoreType.DMA((7,)),
        ],
        smem=1, far=7, flops=10**8, name="prepare",
    )(ids, log_decay, beta, seg_r, *weights)
    same = jnp.concatenate(lax.optimization_barrier((moved[1], moved[2], moved[3], columns))[:3], axis=0)
    other = across(same)
    piece, pre, tail = call(
        project_body,
        [((T, 2048), bf16), ((T, 1024), bf16), ((16, 1024), bf16)],
        smem=1, flops=2 * T * 2048 * 1024, name="project",
    )(ids, tokens, swapped, same, other, w_query_key, w_value)
    tail = lax.ppermute(tail, "ctx", [(i, (i + 1) % 32) for i in range(32)])
    (gate,) = call(gate_body, [((T, 512), f32)], flops=2 * T * 2048 * 512, name="gate")(
        piece, w_gate_out, gain
    )

    pack = ((PACK, 256), bf16)
    *maps, query, key_t, w = call(
        recur_body,
        [pack, pack, pack, pack, ((T, 256), bf16), ((2, 128, T), bf16), ((4, T, 256), bf16)],
        scratch=[pltpu.VMEM((T + 8, 1024), f32), pltpu.VMEM((4, PACK, 256), bf16)],
        smem=1, flops=10**9, name="recur",
    )(ids, pre, tail, conv_query_key, conv_value, columns, decay)
    local_out, edge = call(
        local_body, [((T, 512), f32), ((T, 512), bf16)], flops=2 * 10**8, name="local"
    )(query, key_t, w, columns, decay)

    slots = [pltpu.VMEM((4, PACK, 256), bf16)]
    maps = [maps[0]] + [along_x(maps[s], s) for s in (1, 2, 3)]
    total, before = call(
        group_body, [pack, ((3, PACK, 256), bf16)], scratch=slots, smem=1, name="group"
    )(ids, *maps)
    totals = [total] + [along_z(total, s) for s in (1, 2, 3)]
    start, whole = call(
        depth_body, [((4, PACK, 256), bf16), ((128, 128), bf16)], scratch=slots, smem=1, name="depth"
    )(ids, *totals, before)
    state_shape = ((128, 128), bf16)
    states = call(
        spread_body, [state_shape] * 4, scratch=[pltpu.VMEM((4, 128, 128), bf16)], smem=1, name="spread"
    )(ids, mirrored(whole), start)
    states = [states[0]] + [along_x(states[s], s) for s in (1, 2, 3)]

    normed, his = call(
        output_body,
        [((HALF, 512), bf16), ((HALF, 2048), bf16)],
        scratch=[pltpu.VMEM((4, 128, 128), bf16), pltpu.VMEM((T, 512), bf16)],
        smem=1, flops=2 * HALF * 512 * 2048, name="output",
    )(ids, *states, local_out, edge, gate, w_output)
    got = across(his)
    (mine,) = call(mine_body, [((HALF, 2048), f32)], flops=2 * HALF * 512 * 2048, name="mine")(
        normed, w_output
    )
    part = ((32, 2048), bf16)
    own, *parts = call(pair_body, [((32, 2048), f32), part, part, part], smem=1, name="pair")(
        ids, mine, got
    )
    parts = [along_y(parts[s - 1], s) for s in (1, 2, 3)]
    return call(last_body, [part], name="last")(own, *parts)[0]


def solution(mesh):
    return jax.shard_map(
        local,
        mesh=mesh,
        in_specs=(
            P(("ctx", "tp"), None),
            P(None, None, "tp"),
            P(None, "tp"),
            P(None, "tp"),
            P(None, None, "tp"),
            P(None, "tp"),
            P("tp", "ctx"),
            P("tp", "ctx"),
            P("ctx"),
            P(),
            P("tp", None),
        ),
        out_specs=P(("ctx", "tp"), None),
        check_vma=False,
    )
```

```python
import functools

import jax
import jax.numpy as jnp
from jax import lax
from jax.experimental import pallas as pl
from jax.experimental.pallas import tpu as pltpu
from jax.sharding import PartitionSpec as P


DK = 128
CONV = 4
T = 256
HALF = 128
PACK = 144
f32 = jnp.float32
bf16 = jnp.bfloat16
INTERPRET = False


def mm(a, b):
    return jnp.dot(a.astype(bf16), b.astype(bf16), preferred_element_type=f32)


def mm_exact(a, b):
    return jnp.dot(a, b, preferred_element_type=f32, precision=lax.Precision.HIGHEST)


def call(kernel, outs, scratch=(), smem=0, far=0, vmem=16, flops=0, name=None):
    def run(*args):
        args = [
            pltpu.with_memory_space_constraint(a, pltpu.HBM) if smem <= i < smem + far and not INTERPRET else a
            for i, a in enumerate(args)
        ]
        spaces = [pltpu.SMEM] * smem + [pltpu.HBM] * far + [pltpu.VMEM] * (len(args) - smem - far)
        in_specs = [pl.BlockSpec(memory_space=space) for space in spaces]
        shapes = [jax.ShapeDtypeStruct(s, d) for s, d in outs]
        moved = sum(a.size * a.dtype.itemsize for a in args) + sum(
            s.size * s.dtype.itemsize for s in shapes
        )
        return pl.pallas_call(
            kernel,
            out_shape=shapes,
            in_specs=in_specs,
            out_specs=[pl.BlockSpec(memory_space=pltpu.VMEM)] * len(outs),
            scratch_shapes=list(scratch),
            compiler_params=pltpu.CompilerParams(vmem_limit_bytes=vmem << 20),
            cost_estimate=pl.CostEstimate(flops=flops, bytes_accessed=moved, transcendentals=0),
            interpret=INTERPRET,
            name=name,
        )(*args)

    return run


def silu(v):
    return v / (1.0 + jnp.exp(-v))


def prepare_body(
    ids, ld_far, beta_far, seg_far, w_qk, w_v, w_g, w_o,
    w_qk_near, w_v_near, w_g_near, w_o_near, cols_out, decay_out, ld, beta, seg_r, sems,
):
    pairs = (
        (ld_far, ld), (beta_far, beta), (seg_far, seg_r),
        (w_qk, w_qk_near), (w_v, w_v_near), (w_g, w_g_near), (w_o, w_o_near),
    )
    copies = [pltpu.make_async_copy(src, dst, sems.at[i]) for i, (src, dst) in enumerate(pairs)]
    for copy in copies:
        copy.start()
    for copy in copies[:3]:
        copy.wait()
    first = ids[5].astype(f32)
    seg_row = seg_r[...].astype(f32)
    clipped = jnp.maximum(ld[...], -120.0)
    rows = lax.broadcasted_iota(jnp.int32, (T, T), 0)
    cols = lax.broadcasted_iota(jnp.int32, (T, T), 1)
    gam_row = mm_exact(
        jnp.concatenate([clipped, jnp.zeros((4, T), f32)], axis=0), (rows <= cols).astype(f32)
    )
    gam_col = gam_row.T[:, :4]
    columns = jnp.concatenate([beta[...], jnp.broadcast_to(seg_row, (4, T))], axis=0).T
    beta_col, seg_col = columns[:, :4], columns[:, 4:5]
    lead = jnp.exp(gam_col) * (seg_col < first).astype(f32)
    same_end = seg_col == seg_row[:, T - 1 :]
    to_end = jnp.exp(jnp.where(same_end, gam_col[T - 1 :] - gam_col, -1e30))
    cols_out[...] = jnp.concatenate([beta_col, lead, to_end, jnp.broadcast_to(seg_col, (T, 4))], axis=1)
    within = jnp.logical_and(rows >= cols, seg_col == seg_row)
    for h in range(4):
        decay_out[h] = jnp.exp(jnp.where(within, gam_col[:, h : h + 1] - gam_row[h : h + 1], -1e30))
    for copy in copies[3:]:
        copy.wait()


def gather_body(ids, x0, c0, same, other, piece):
    y, core = ids[3], ids[4]
    for s in range(4):
        chunk = 2 * lax.rem(y + 4 - s, 4)
        rows = slice(32 * s - 32, 32 * s)
        near = same[rows, :] if s else x0[...]
        far = other[rows, :] if s else c0[...]
        piece[pl.ds(pl.multiple_of((chunk + core) * 32, 32), 32), :] = near
        piece[pl.ds(pl.multiple_of((chunk + 1 - core) * 32, 32), 32), :] = far


def project_body(
    ids, x0, c0, same, other, w_qk, w_v, piece, pre, tail
):
    gather_body(ids, x0, c0, same, other, piece)
    x = piece[...]
    for col, w in ((0, w_qk[0]), (256, w_qk[1]), (512, w_v[:, :256]), (768, w_v[:, 256:])):
        out = jnp.dot(x, w, preferred_element_type=f32).astype(bf16)
        pre[:, col : col + 256] = out
        tail[:, col : col + 256] = out[T - 16 :]


def gate_body(piece, w_g, gain, gate):
    x = piece[...]
    for col in (0, 256):
        lin = jnp.dot(x, w_g[:, col : col + 256], preferred_element_type=f32)
        act = silu(lin)
        for k in (0, 128):
            gate[:, col + k : col + k + 128] = act[:, k : k + 128] * gain[...]


def put_map(ref, both, scale):
    ref[0:128, :] = both.astype(bf16)
    hi = scale.astype(bf16).astype(f32)
    mid = (scale - hi).astype(bf16).astype(f32)
    low = scale - hi - mid
    row = lax.broadcasted_iota(jnp.int32, (16, 256), 0)
    ref[128:144, :] = jnp.where(
        row == 0, hi, jnp.where(row == 1, mid, jnp.where(row == 2, low, 0.0))
    ).astype(bf16)


def get_map(ref):
    both = ref[0:128, :].astype(f32)
    scale = jnp.sum(ref[128:144, 0:1].astype(f32), axis=0, keepdims=True)
    return both, scale


def compose(earlier, later):
    both1, scale1 = earlier
    both2, scale2 = later
    cross = mm(both2[:, 128:], both1)
    b = scale2 * both1[:, :128] + both2[:, :128] - cross[:, :128]
    n = scale2 * both1[:, 128:] + scale1 * both2[:, 128:] - cross[:, 128:]
    return jnp.concatenate([b, n], axis=1), scale1 * scale2


def apply_map(both, scale, state):
    return scale * state - mm(both[:, 128:], state) + both[:, :128]


def recur_body(
    ids, pre, tail, taps_qk, taps_v, columns, decay,
    m0, m1, m2, m3, q_out, kt_out, w_out,
    ext, maps,
):
    first = ids[5]
    x_id = ids[1]
    for g in range(8):
        ext[g, 0:8, :] = tail[8:16, 128 * g : 128 * g + 128].astype(f32)
        ext[g, 8 : 8 + T, :] = pre[:, 128 * g : 128 * g + 128].astype(f32)
    age = (first + lax.broadcasted_iota(jnp.int32, (T, 1), 0)).astype(f32) - columns[:, 12:13]
    valid = [
        jnp.broadcast_to((age >= CONV - 1 - j).astype(f32), (T, 128)) for j in range(CONV)
    ]

    def conv(col, taps):
        g = col // 128
        total = ext[g, 8 : 8 + T, :] * taps[CONV - 1 : CONV]
        for j in range(CONV - 1):
            total = total + ext[g, 5 + j : 5 + j + T, :] * taps[j : j + 1] * valid[j]
        return silu(total)

    def unit(v):
        return v * lax.rsqrt(jnp.sum(v * v, axis=1, keepdims=True) + 1e-06)

    keys, keys_t, grams = [], [], []
    for g in range(2):
        q_out[:, 128 * g : 128 * g + 128] = (unit(conv(128 * g, taps_qk[0, :, 128 * g : 128 * g + 128])) * DK ** (-0.5)).astype(bf16)
        key = unit(conv(256 + 128 * g, taps_qk[1, :, 128 * g : 128 * g + 128]))
        key_t = key.T.astype(bf16)
        kt_out[g] = key_t
        keys.append(key)
        keys_t.append(key_t)
        grams.append(mm(key, key_t))

    r1 = lax.broadcasted_iota(jnp.int32, (HALF, HALF), 0)
    c1 = lax.broadcasted_iota(jnp.int32, (HALF, HALF), 1)
    gap = jnp.bitwise_xor(r1, c1)
    low = r1 > c1
    unit_mat = (r1 == c1).astype(f32)
    mats = [columns[:, h : h + 1] * grams[h // 2] * decay[h] for h in range(4)]
    blocks = [mats[h][i : i + HALF, i : i + HALF] for h in range(4) for i in (0, HALF)]
    inverse = [unit_mat - jnp.where(jnp.logical_and(low, gap == 1), a, 0.0) for a in blocks]
    size = 2
    while size < HALF:
        at = jnp.logical_and(low, jnp.logical_and(gap >= size, gap < 2 * size))
        left = [mm(x, jnp.where(at, a, 0.0)) for x, a in zip(inverse, blocks)]
        inverse = [x - mm(y, x) for x, y in zip(inverse, left)]
        size *= 2
    values = [conv(512 + 128 * h, taps_v[:, 128 * h : 128 * h + 128]) for h in range(4)]
    rhs = []
    for h in range(4):
        bet, lead = columns[:, h : h + 1], columns[:, 4 + h : 5 + h]
        rhs.append(jnp.concatenate([bet * values[h], (bet * lead) * keys[h // 2]], axis=1))
    top = [mm(inverse[2 * h], rhs[h][:HALF]) for h in range(4)]
    low_rhs = [rhs[h][HALF:] - mm(mats[h][HALF:, :HALF], top[h]) for h in range(4)]
    bottom = [mm(inverse[2 * h + 1], low_rhs[h]) for h in range(4)]
    solved = [jnp.concatenate([top[h], bottom[h]], axis=0) for h in range(4)]
    both = [mm(keys_t[h // 2], solved[h] * columns[:, 8 + h : 9 + h]) for h in range(4)]
    for h in range(4):
        put_map(maps.at[h], both[h], columns[T - 1 : T, 4 + h : 5 + h])
        w_out[h] = solved[h].astype(bf16)
    for s, out in enumerate((m0, m1, m2, m3)):
        out[...] = maps[jnp.bitwise_xor(x_id, s)]


def local_body(q, k_t, w, columns, decay, local, edge):
    for g in range(2):
        query = q[:, 128 * g : 128 * g + 128]
        dots = jnp.dot(query, k_t[g], preferred_element_type=f32)
        for h in (2 * g, 2 * g + 1):
            p = dots * decay[h]
            both = jnp.dot(p.astype(bf16), w[h], preferred_element_type=f32)
            cols = slice(128 * h, 128 * h + 128)
            local[:, cols] = both[:, :128]
            edge[:, cols] = (columns[:, 4 + h : 5 + h] * query.astype(f32) - both[:, 128:]).astype(bf16)


def group_body(ids, p0, p1, p2, p3, total, before, slots):
    x = ids[1]
    for s, p in enumerate((p0, p1, p2, p3)):
        slots[s] = p[...]
    acc = get_map(slots.at[x])
    put_map(before.at[0], *acc)
    for j in range(1, 4):
        acc = compose(acc, get_map(slots.at[jnp.bitwise_xor(x, j)]))
        put_map(before.at[j] if j < 3 else total, *acc)


def depth_body(ids, p0, p1, p2, p3, before, start, whole, slots):
    z = ids[2]
    for s, p in enumerate((p0, p1, p2, p3)):
        slots[s] = p[...]
    acc = get_map(slots.at[z])
    zero = jnp.zeros((128, 256), f32)
    both = jnp.where(z > 0, acc[0], zero)
    scale = jnp.where(z > 0, acc[1], jnp.ones((1, 1), f32))
    for j in range(1, 4):
        acc = compose(acc, get_map(slots.at[jnp.bitwise_xor(z, j)]))
        if j < 3:
            both = jnp.where(z > j, acc[0], both)
            scale = jnp.where(z > j, acc[1], scale)
    whole[...] = acc[0][:, :128].astype(bf16)
    put_map(start.at[0], both, scale)
    for j in range(3):
        put_map(start.at[j + 1], *compose((both, scale), get_map(before.at[j])))


def spread_body(ids, state, start, s0, s1, s2, s3, slots):
    x = ids[1]
    incoming = jnp.where(ids[6] > 0, state[...].astype(f32), 0.0)
    for j in range(4):
        slots[j] = apply_map(*get_map(start.at[j]), incoming).astype(bf16)
    for s, out in enumerate((s0, s1, s2, s3)):
        out[...] = slots[jnp.bitwise_xor(x, s)]


def output_body(ids, s0, s1, s2, s3, local, edge, gate, w_o, mine, his, slots, normed):
    x, core = ids[1], ids[4]
    for s, p in enumerate((s0, s1, s2, s3)):
        slots[s] = p[...]
    for h in range(4):
        cols = slice(128 * h, 128 * h + 128)
        state = slots[jnp.bitwise_xor(x, h)]
        out = local[:, cols] + jnp.dot(edge[:, cols], state, preferred_element_type=f32)
        scale = lax.rsqrt(jnp.mean(out * out, axis=1, keepdims=True) + 1e-06)
        normed[:, cols] = (out * scale * gate[:, cols]).astype(bf16)
    for y in range(4):
        mine[32 * y : 32 * y + 32, :] = normed[pl.ds(pl.multiple_of((2 * y + core) * 32, 32), 32), :]
    other = jnp.concatenate(
        [normed[pl.ds(pl.multiple_of((2 * y + 1 - core) * 32, 32), 32), :] for y in range(4)], axis=0
    )
    for col in range(0, 2048, 256):
        his[:, col : col + 256] = jnp.dot(
            other, w_o[:, col : col + 256], preferred_element_type=f32
        ).astype(bf16)


def mine_body(normed, w_o, out):
    x = normed[...]
    for col in range(0, 2048, 256):
        out[:, col : col + 256] = jnp.dot(x, w_o[:, col : col + 256], preferred_element_type=f32)


def pair_body(ids, mine, got, own, o1, o2, o3):
    y = ids[3]

    def summed(d):
        at = pl.ds(pl.multiple_of(lax.rem(y + d, 4) * 32, 32), 32)
        return mine[at, :] + got[at, :].astype(f32)

    own[...] = summed(0)
    for d, out in ((1, o1), (2, o2), (3, o3)):
        out[...] = summed(d).astype(bf16)


def last_body(own, r1, r2, r3, out):
    out[...] = (
        own[...] + r1[...].astype(f32) + r2[...].astype(f32) + r3[...].astype(f32)
    ).astype(bf16)


def along_y(array, s):
    pairs = [(2 * y + k, 2 * ((y + s) % 4) + k) for y in range(4) for k in range(2)]
    return lax.ppermute(array, "tp", pairs)


def across(array):
    return lax.ppermute(array, "tp", [(i, i ^ 1) for i in range(8)])


def along_x(array, s):
    pairs = [(4 * z + x, 4 * z + (x ^ s)) for z in range(8) for x in range(4)]
    return lax.ppermute(array, "ctx", pairs)


def along_z(array, s):
    pairs = [
        (16 * g + 4 * z + x, 16 * g + 4 * (z ^ s) + x)
        for g in range(2)
        for z in range(4)
        for x in range(4)
    ]
    return lax.ppermute(array, "ctx", pairs)


def mirrored(array):
    pairs = [(4 * z + x, 4 * (7 - z) + x) for z in range(8) for x in range(4)]
    return lax.ppermute(array, "ctx", pairs)


def local(
    tokens, w_query_key, w_value, w_gate_out, conv_query_key, conv_value,
    log_decay, beta, seg_start, norm_gain, w_output,
):
    ctx = lax.axis_index("ctx")
    tp = lax.axis_index("tp")
    ids = jnp.stack(
        [ctx, ctx % 4, (ctx // 4) % 4, tp // 2, tp % 2, ctx * T, ctx // 16, tp]
    ).astype(jnp.int32)
    seg_r = seg_start.reshape(1, T)
    gain = norm_gain.reshape(1, 128)
    near = lambda a: (a.shape, a.dtype)

    moved = {s: along_y(tokens, s) for s in (2, 1, 3)}
    swapped = across(tokens)
    weights = (w_query_key, w_value, w_gate_out, w_output)
    w_query_key, w_value, w_gate_out, w_output, columns, decay = call(
        prepare_body,
        [near(w) for w in weights] + [((T, 16), f32), ((4, T, T), f32)],
        scratch=[
            pltpu.VMEM((4, T), f32), pltpu.VMEM((4, T), f32), pltpu.VMEM((1, T), jnp.int32),
            pltpu.SemaphoreType.DMA((7,)),
        ],
        smem=1, far=7, flops=10**8, name="prepare",
    )(ids, log_decay, beta, seg_r, *weights)
    same = jnp.concatenate(lax.optimization_barrier((moved[1], moved[2], moved[3], columns))[:3], axis=0)
    other = across(same)
    piece, pre, tail = call(
        project_body,
        [((T, 2048), bf16), ((T, 1024), bf16), ((16, 1024), bf16)],
        smem=1, flops=2 * T * 2048 * 1024, name="project",
    )(ids, tokens, swapped, same, other, w_query_key, w_value)
    tail = lax.ppermute(tail, "ctx", [(i, (i + 1) % 32) for i in range(32)])
    (gate,) = call(gate_body, [((T, 512), f32)], flops=2 * T * 2048 * 512, name="gate")(
        piece, w_gate_out, gain
    )

    pack = ((PACK, 256), bf16)
    *maps, query, key_t, w = call(
        recur_body,
        [pack, pack, pack, pack, ((T, 256), bf16), ((2, 128, T), bf16), ((4, T, 256), bf16)],
        scratch=[pltpu.VMEM((8, T + 8, 128), f32), pltpu.VMEM((4, PACK, 256), bf16)],
        smem=1, flops=10**9, name="recur",
    )(ids, pre, tail, conv_query_key, conv_value, columns, decay)
    local_out, edge = call(
        local_body, [((T, 512), f32), ((T, 512), bf16)], flops=2 * 10**8, name="local"
    )(query, key_t, w, columns, decay)

    slots = [pltpu.VMEM((4, PACK, 256), bf16)]
    maps = [maps[0]] + [along_x(maps[s], s) for s in (1, 2, 3)]
    total, before = call(
        group_body, [pack, ((3, PACK, 256), bf16)], scratch=slots, smem=1, name="group"
    )(ids, *maps)
    totals = [total] + [along_z(total, s) for s in (1, 2, 3)]
    start, whole = call(
        depth_body, [((4, PACK, 256), bf16), ((128, 128), bf16)], scratch=slots, smem=1, name="depth"
    )(ids, *totals, before)
    state_shape = ((128, 128), bf16)
    states = call(
        spread_body, [state_shape] * 4, scratch=[pltpu.VMEM((4, 128, 128), bf16)], smem=1, name="spread"
    )(ids, mirrored(whole), start)
    states = [states[0]] + [along_x(states[s], s) for s in (1, 2, 3)]

    normed, his = call(
        output_body,
        [((HALF, 512), bf16), ((HALF, 2048), bf16)],
        scratch=[pltpu.VMEM((4, 128, 128), bf16), pltpu.VMEM((T, 512), bf16)],
        smem=1, flops=2 * HALF * 512 * 2048, name="output",
    )(ids, *states, local_out, edge, gate, w_output)
    got = across(his)
    (mine,) = call(mine_body, [((HALF, 2048), f32)], flops=2 * HALF * 512 * 2048, name="mine")(
        normed, w_output
    )
    part = ((32, 2048), bf16)
    own, *parts = call(pair_body, [((32, 2048), f32), part, part, part], smem=1, name="pair")(
        ids, mine, got
    )
    parts = [along_y(parts[s - 1], s) for s in (1, 2, 3)]
    return call(last_body, [part], name="last")(own, *parts)[0]


def solution(mesh):
    return jax.shard_map(
        local,
        mesh=mesh,
        in_specs=(
            P(("ctx", "tp"), None),
            P(None, None, "tp"),
            P(None, "tp"),
            P(None, "tp"),
            P(None, None, "tp"),
            P(None, "tp"),
            P("tp", "ctx"),
            P("tp", "ctx"),
            P("ctx"),
            P(),
            P("tp", None),
        ),
        out_specs=P(("ctx", "tp"), None),
        check_vma=False,
    )
```

```python
import functools

import jax
import jax.numpy as jnp
from jax import lax
from jax.experimental import pallas as pl
from jax.experimental.pallas import tpu as pltpu
from jax.sharding import PartitionSpec as P


DK = 128
CONV = 4
T = 256
HALF = 128
PACK = 136
f32 = jnp.float32
bf16 = jnp.bfloat16
INTERPRET = False


def mm(a, b):
    return jnp.dot(a.astype(bf16), b.astype(bf16), preferred_element_type=f32)


def mm_exact(a, b):
    return jnp.dot(a, b, preferred_element_type=f32, precision=lax.Precision.HIGHEST)


def call(kernel, outs, scratch=(), smem=0, far=0, vmem=16, flops=0, name=None):
    def run(*args):
        args = [
            pltpu.with_memory_space_constraint(a, pltpu.HBM) if smem <= i < smem + far and not INTERPRET else a
            for i, a in enumerate(args)
        ]
        spaces = [pltpu.SMEM] * smem + [pltpu.HBM] * far + [pltpu.VMEM] * (len(args) - smem - far)
        in_specs = [pl.BlockSpec(memory_space=space) for space in spaces]
        shapes = [jax.ShapeDtypeStruct(s, d) for s, d in outs]
        moved = sum(a.size * a.dtype.itemsize for a in args) + sum(
            s.size * s.dtype.itemsize for s in shapes
        )
        return pl.pallas_call(
            kernel,
            out_shape=shapes,
            in_specs=in_specs,
            out_specs=[pl.BlockSpec(memory_space=pltpu.VMEM)] * len(outs),
            scratch_shapes=list(scratch),
            compiler_params=pltpu.CompilerParams(vmem_limit_bytes=vmem << 20),
            cost_estimate=pl.CostEstimate(flops=flops, bytes_accessed=moved, transcendentals=0),
            interpret=INTERPRET,
            name=name,
        )(*args)

    return run


def silu(v):
    return v / (1.0 + jnp.exp(-v))


def prepare_body(
    ids, ld_far, beta_far, seg_far, w_qk, w_v, w_g, w_o,
    w_qk_near, w_v_near, w_g_near, w_o_near, cols_out, decay_out, ld, beta, seg_r, sems,
):
    pairs = (
        (ld_far, ld), (beta_far, beta), (seg_far, seg_r),
        (w_qk, w_qk_near), (w_v, w_v_near), (w_g, w_g_near), (w_o, w_o_near),
    )
    copies = [pltpu.make_async_copy(src, dst, sems.at[i]) for i, (src, dst) in enumerate(pairs)]
    for copy in copies:
        copy.start()
    for copy in copies[:3]:
        copy.wait()
    first = ids[5].astype(f32)
    seg_row = seg_r[...].astype(f32)
    clipped = jnp.maximum(ld[...], -120.0)
    rows = lax.broadcasted_iota(jnp.int32, (T, T), 0)
    cols = lax.broadcasted_iota(jnp.int32, (T, T), 1)
    gam_row = mm_exact(
        jnp.concatenate([clipped, jnp.zeros((4, T), f32)], axis=0), (rows <= cols).astype(f32)
    )
    gam_col = gam_row.T[:, :4]
    columns = jnp.concatenate([beta[...], jnp.broadcast_to(seg_row, (4, T))], axis=0).T
    beta_col, seg_col = columns[:, :4], columns[:, 4:5]
    lead = jnp.exp(gam_col) * (seg_col < first).astype(f32)
    same_end = seg_col == seg_row[:, T - 1 :]
    to_end = jnp.exp(jnp.where(same_end, gam_col[T - 1 :] - gam_col, -1e30))
    cols_out[...] = jnp.concatenate([beta_col, lead, to_end, jnp.broadcast_to(seg_col, (T, 4))], axis=1)
    within = jnp.logical_and(rows >= cols, seg_col == seg_row)
    for h in range(4):
        decay_out[h] = jnp.exp(jnp.where(within, gam_col[:, h : h + 1] - gam_row[h : h + 1], -1e30))
    for copy in copies[3:]:
        copy.wait()


def gather_body(ids, x0, c0, same, other, piece):
    y, core = ids[3], ids[4]
    for s in range(4):
        chunk = 2 * lax.rem(y + 4 - s, 4)
        rows = slice(32 * s - 32, 32 * s)
        near = same[rows, :] if s else x0[...]
        far = other[rows, :] if s else c0[...]
        piece[pl.ds(pl.multiple_of((chunk + core) * 32, 32), 32), :] = near
        piece[pl.ds(pl.multiple_of((chunk + 1 - core) * 32, 32), 32), :] = far


def project_body(
    ids, x0, c0, same, other, w_qk, w_v, piece, pre, tail
):
    gather_body(ids, x0, c0, same, other, piece)
    x = piece[...]
    for col, w in ((0, w_qk[0]), (256, w_qk[1]), (512, w_v[:, :256]), (768, w_v[:, 256:])):
        out = jnp.dot(x, w, preferred_element_type=f32).astype(bf16)
        pre[:, col : col + 256] = out
        tail[:, col : col + 256] = out[T - 16 :]


def gate_body(piece, w_g, gain, gate):
    x = piece[...]
    for col in (0, 256):
        lin = jnp.dot(x, w_g[:, col : col + 256], preferred_element_type=f32)
        act = silu(lin)
        for k in (0, 128):
            gate[:, col + k : col + k + 128] = act[:, k : k + 128] * gain[...]


def put_map(ref, both, scale):
    ref[0:128, :] = both.astype(bf16)
    hi = scale.astype(bf16).astype(f32)
    mid = (scale - hi).astype(bf16).astype(f32)
    low = scale - hi - mid
    row = lax.broadcasted_iota(jnp.int32, (8, 256), 0)
    ref[128:136, :] = jnp.where(
        row == 0, hi, jnp.where(row == 1, mid, jnp.where(row == 2, low, 0.0))
    ).astype(bf16)


def get_map(ref):
    both = ref[0:128, :].astype(f32)
    scale = jnp.sum(ref[128:136, 0:1].astype(f32), axis=0, keepdims=True)
    return both, scale


def compose(earlier, later):
    both1, scale1 = earlier
    both2, scale2 = later
    cross = mm(both2[:, 128:], both1)
    b = scale2 * both1[:, :128] + both2[:, :128] - cross[:, :128]
    n = scale2 * both1[:, 128:] + scale1 * both2[:, 128:] - cross[:, 128:]
    return jnp.concatenate([b, n], axis=1), scale1 * scale2


def apply_map(both, scale, state):
    return scale * state - mm(both[:, 128:], state) + both[:, :128]


def recur_body(
    ids, pre, tail, taps_qk, taps_v, columns, decay,
    m0, m1, m2, m3, q_out, kt_out, w_out,
    ext, maps,
):
    first = ids[5]
    x_id = ids[1]
    for g in range(8):
        ext[g, 0:8, :] = tail[8:16, 128 * g : 128 * g + 128].astype(f32)
        ext[g, 8 : 8 + T, :] = pre[:, 128 * g : 128 * g + 128].astype(f32)
    age = (first + lax.broadcasted_iota(jnp.int32, (T, 1), 0)).astype(f32) - columns[:, 12:13]
    valid = [
        jnp.broadcast_to((age >= CONV - 1 - j).astype(f32), (T, 128)) for j in range(CONV)
    ]

    def conv(col, taps):
        g = col // 128
        total = ext[g, 8 : 8 + T, :] * taps[CONV - 1 : CONV]
        for j in range(CONV - 1):
            total = total + ext[g, 5 + j : 5 + j + T, :] * taps[j : j + 1] * valid[j]
        return silu(total)

    def unit(v):
        return v * lax.rsqrt(jnp.sum(v * v, axis=1, keepdims=True) + 1e-06)

    keys, keys_t, grams = [], [], []
    for g in range(2):
        q_out[:, 128 * g : 128 * g + 128] = (unit(conv(128 * g, taps_qk[0, :, 128 * g : 128 * g + 128])) * DK ** (-0.5)).astype(bf16)
        key = unit(conv(256 + 128 * g, taps_qk[1, :, 128 * g : 128 * g + 128]))
        key_t = key.T.astype(bf16)
        kt_out[g] = key_t
        keys.append(key)
        keys_t.append(key_t)
        grams.append(mm(key, key_t))

    r1 = lax.broadcasted_iota(jnp.int32, (HALF, HALF), 0)
    c1 = lax.broadcasted_iota(jnp.int32, (HALF, HALF), 1)
    gap = jnp.bitwise_xor(r1, c1)
    low = r1 > c1
    unit_mat = (r1 == c1).astype(f32)
    mats = [columns[:, h : h + 1] * grams[h // 2] * decay[h] for h in range(4)]
    blocks = [mats[h][i : i + HALF, i : i + HALF] for h in range(4) for i in (0, HALF)]
    inverse = [unit_mat - jnp.where(jnp.logical_and(low, gap == 1), a, 0.0) for a in blocks]
    size = 2
    while size < HALF:
        at = jnp.logical_and(low, jnp.logical_and(gap >= size, gap < 2 * size))
        left = [mm(x, jnp.where(at, a, 0.0)) for x, a in zip(inverse, blocks)]
        inverse = [x - mm(y, x) for x, y in zip(inverse, left)]
        size *= 2
    values = [conv(512 + 128 * h, taps_v[:, 128 * h : 128 * h + 128]) for h in range(4)]
    rhs = []
    for h in range(4):
        bet, lead = columns[:, h : h + 1], columns[:, 4 + h : 5 + h]
        rhs.append(jnp.concatenate([bet * values[h], (bet * lead) * keys[h // 2]], axis=1))
    top = [mm(inverse[2 * h], rhs[h][:HALF]) for h in range(4)]
    low_rhs = [rhs[h][HALF:] - mm(mats[h][HALF:, :HALF], top[h]) for h in range(4)]
    bottom = [mm(inverse[2 * h + 1], low_rhs[h]) for h in range(4)]
    solved = [jnp.concatenate([top[h], bottom[h]], axis=0) for h in range(4)]
    both = [mm(keys_t[h // 2], solved[h] * columns[:, 8 + h : 9 + h]) for h in range(4)]
    for h in range(4):
        put_map(maps.at[h], both[h], columns[T - 1 : T, 4 + h : 5 + h])
        w_out[h] = solved[h].astype(bf16)
    for s, out in enumerate((m0, m1, m2, m3)):
        out[...] = maps[jnp.bitwise_xor(x_id, s)]


def local_body(q, k_t, w, columns, decay, local, edge):
    for g in range(2):
        query = q[:, 128 * g : 128 * g + 128]
        dots = jnp.dot(query, k_t[g], preferred_element_type=f32)
        for h in (2 * g, 2 * g + 1):
            p = dots * decay[h]
            both = jnp.dot(p.astype(bf16), w[h], preferred_element_type=f32)
            cols = slice(128 * h, 128 * h + 128)
            local[:, cols] = both[:, :128]
            edge[:, cols] = (columns[:, 4 + h : 5 + h] * query.astype(f32) - both[:, 128:]).astype(bf16)


def group_body(ids, p0, p1, p2, p3, total, before, slots):
    x = ids[1]
    for s, p in enumerate((p0, p1, p2, p3)):
        slots[s] = p[...]
    acc = get_map(slots.at[x])
    put_map(before.at[0], *acc)
    for j in range(1, 4):
        acc = compose(acc, get_map(slots.at[jnp.bitwise_xor(x, j)]))
        put_map(before.at[j] if j < 3 else total, *acc)


def depth_body(ids, p0, p1, p2, p3, before, start, whole, slots):
    z = ids[2]
    for s, p in enumerate((p0, p1, p2, p3)):
        slots[s] = p[...]
    acc = get_map(slots.at[z])
    zero = jnp.zeros((128, 256), f32)
    both = jnp.where(z > 0, acc[0], zero)
    scale = jnp.where(z > 0, acc[1], jnp.ones((1, 1), f32))
    for j in range(1, 4):
        acc = compose(acc, get_map(slots.at[jnp.bitwise_xor(z, j)]))
        if j < 3:
            both = jnp.where(z > j, acc[0], both)
            scale = jnp.where(z > j, acc[1], scale)
    whole[...] = acc[0][:, :128].astype(bf16)
    put_map(start.at[0], both, scale)
    for j in range(3):
        put_map(start.at[j + 1], *compose((both, scale), get_map(before.at[j])))


def spread_body(ids, state, start, s0, s1, s2, s3, slots):
    x = ids[1]
    incoming = jnp.where(ids[6] > 0, state[...].astype(f32), 0.0)
    for j in range(4):
        slots[j] = apply_map(*get_map(start.at[j]), incoming).astype(bf16)
    for s, out in enumerate((s0, s1, s2, s3)):
        out[...] = slots[jnp.bitwise_xor(x, s)]


def output_body(ids, s0, s1, s2, s3, local, edge, gate, w_o, mine, his, slots, normed):
    x, core = ids[1], ids[4]
    for s, p in enumerate((s0, s1, s2, s3)):
        slots[s] = p[...]
    for h in range(4):
        cols = slice(128 * h, 128 * h + 128)
        state = slots[jnp.bitwise_xor(x, h)]
        out = local[:, cols] + jnp.dot(edge[:, cols], state, preferred_element_type=f32)
        scale = lax.rsqrt(jnp.mean(out * out, axis=1, keepdims=True) + 1e-06)
        normed[:, cols] = (out * scale * gate[:, cols]).astype(bf16)
    for y in range(4):
        mine[32 * y : 32 * y + 32, :] = normed[pl.ds(pl.multiple_of((2 * y + core) * 32, 32), 32), :]
    other = jnp.concatenate(
        [normed[pl.ds(pl.multiple_of((2 * y + 1 - core) * 32, 32), 32), :] for y in range(4)], axis=0
    )
    for col in range(0, 2048, 256):
        his[:, col : col + 256] = jnp.dot(
            other, w_o[:, col : col + 256], preferred_element_type=f32
        ).astype(bf16)


def mine_body(normed, w_o, out):
    x = normed[...]
    for col in range(0, 2048, 256):
        out[:, col : col + 256] = jnp.dot(x, w_o[:, col : col + 256], preferred_element_type=f32)


def pair_body(ids, mine, got, own, o1, o2, o3):
    y = ids[3]

    def summed(d):
        at = pl.ds(pl.multiple_of(lax.rem(y + d, 4) * 32, 32), 32)
        return mine[at, :] + got[at, :].astype(f32)

    own[...] = summed(0)
    for d, out in ((1, o1), (2, o2), (3, o3)):
        out[...] = summed(d).astype(bf16)


def last_body(own, r1, r2, r3, out):
    out[...] = (
        own[...] + r1[...].astype(f32) + r2[...].astype(f32) + r3[...].astype(f32)
    ).astype(bf16)


def along_y(array, s):
    pairs = [(2 * y + k, 2 * ((y + s) % 4) + k) for y in range(4) for k in range(2)]
    return lax.ppermute(array, "tp", pairs)


def across(array):
    return lax.ppermute(array, "tp", [(i, i ^ 1) for i in range(8)])


def along_x(array, s):
    pairs = [(4 * z + x, 4 * z + (x ^ s)) for z in range(8) for x in range(4)]
    return lax.ppermute(array, "ctx", pairs)


def along_z(array, s):
    pairs = [
        (16 * g + 4 * z + x, 16 * g + 4 * (z ^ s) + x)
        for g in range(2)
        for z in range(4)
        for x in range(4)
    ]
    return lax.ppermute(array, "ctx", pairs)


def mirrored(array):
    pairs = [(4 * z + x, 4 * (7 - z) + x) for z in range(8) for x in range(4)]
    return lax.ppermute(array, "ctx", pairs)


def local(
    tokens, w_query_key, w_value, w_gate_out, conv_query_key, conv_value,
    log_decay, beta, seg_start, norm_gain, w_output,
):
    ctx = lax.axis_index("ctx")
    tp = lax.axis_index("tp")
    ids = jnp.stack(
        [ctx, ctx % 4, (ctx // 4) % 4, tp // 2, tp % 2, ctx * T, ctx // 16, tp]
    ).astype(jnp.int32)
    seg_r = seg_start.reshape(1, T)
    gain = norm_gain.reshape(1, 128)
    near = lambda a: (a.shape, a.dtype)

    moved = {s: along_y(tokens, s) for s in (2, 1, 3)}
    swapped = across(tokens)
    weights = (w_query_key, w_value, w_gate_out, w_output)
    w_query_key, w_value, w_gate_out, w_output, columns, decay = call(
        prepare_body,
        [near(w) for w in weights] + [((T, 16), f32), ((4, T, T), f32)],
        scratch=[
            pltpu.VMEM((4, T), f32), pltpu.VMEM((4, T), f32), pltpu.VMEM((1, T), jnp.int32),
            pltpu.SemaphoreType.DMA((7,)),
        ],
        smem=1, far=7, flops=10**8, name="prepare",
    )(ids, log_decay, beta, seg_r, *weights)
    same = jnp.concatenate(lax.optimization_barrier((moved[1], moved[2], moved[3], columns))[:3], axis=0)
    other = across(same)
    piece, pre, tail = call(
        project_body,
        [((T, 2048), bf16), ((T, 1024), bf16), ((16, 1024), bf16)],
        smem=1, flops=2 * T * 2048 * 1024, name="project",
    )(ids, tokens, swapped, same, other, w_query_key, w_value)
    tail = lax.ppermute(tail, "ctx", [(i, (i + 1) % 32) for i in range(32)])
    (gate,) = call(gate_body, [((T, 512), f32)], flops=2 * T * 2048 * 512, name="gate")(
        piece, w_gate_out, gain
    )

    pack = ((PACK, 256), bf16)
    *maps, query, key_t, w = call(
        recur_body,
        [pack, pack, pack, pack, ((T, 256), bf16), ((2, 128, T), bf16), ((4, T, 256), bf16)],
        scratch=[pltpu.VMEM((8, T + 8, 128), f32), pltpu.VMEM((4, PACK, 256), bf16)],
        smem=1, flops=10**9, name="recur",
    )(ids, pre, tail, conv_query_key, conv_value, columns, decay)
    local_out, edge = call(
        local_body, [((T, 512), f32), ((T, 512), bf16)], flops=2 * 10**8, name="local"
    )(query, key_t, w, columns, decay)

    slots = [pltpu.VMEM((4, PACK, 256), bf16)]
    maps = [maps[0]] + [along_x(maps[s], s) for s in (1, 2, 3)]
    total, before = call(
        group_body, [pack, ((3, PACK, 256), bf16)], scratch=slots, smem=1, name="group"
    )(ids, *maps)
    totals = [total] + [along_z(total, s) for s in (1, 2, 3)]
    start, whole = call(
        depth_body, [((4, PACK, 256), bf16), ((128, 128), bf16)], scratch=slots, smem=1, name="depth"
    )(ids, *totals, before)
    state_shape = ((128, 128), bf16)
    states = call(
        spread_body, [state_shape] * 4, scratch=[pltpu.VMEM((4, 128, 128), bf16)], smem=1, name="spread"
    )(ids, mirrored(whole), start)
    states = [states[0]] + [along_x(states[s], s) for s in (1, 2, 3)]

    normed, his = call(
        output_body,
        [((HALF, 512), bf16), ((HALF, 2048), bf16)],
        scratch=[pltpu.VMEM((4, 128, 128), bf16), pltpu.VMEM((T, 512), bf16)],
        smem=1, flops=2 * HALF * 512 * 2048, name="output",
    )(ids, *states, local_out, edge, gate, w_output)
    got = across(his)
    (mine,) = call(mine_body, [((HALF, 2048), f32)], flops=2 * HALF * 512 * 2048, name="mine")(
        normed, w_output
    )
    part = ((32, 2048), bf16)
    own, *parts = call(pair_body, [((32, 2048), f32), part, part, part], smem=1, name="pair")(
        ids, mine, got
    )
    parts = [along_y(parts[s - 1], s) for s in (1, 2, 3)]
    return call(last_body, [part], name="last")(own, *parts)[0]


def solution(mesh):
    return jax.shard_map(
        local,
        mesh=mesh,
        in_specs=(
            P(("ctx", "tp"), None),
            P(None, None, "tp"),
            P(None, "tp"),
            P(None, "tp"),
            P(None, None, "tp"),
            P(None, "tp"),
            P("tp", "ctx"),
            P("tp", "ctx"),
            P("ctx"),
            P(),
            P("tp", None),
        ),
        out_specs=P(("ctx", "tp"), None),
        check_vma=False,
    )
```
